32 devices in a mesh: groups: 2 (over y), seq: 4 (over z), chan: 4 (over x, core).
Axes of the slice: x: 2, y: 2, z: 4, core: 2. Of those that a mesh axis runs over, the one named last changes fastest.
Arguments:
- dna_bases: int32 [4096], P(('groups', 'seq')), parts along dimension 0, may hold values from 0 to 3
- w_stem: bfloat16 [768, 5, 4], P('chan'), may hold values from -2.5 to 2.5
- w_enc: bfloat16 [1536, 5, 768], P(None, None, 'chan'), may hold values from -0.09375 to 0.09375
- w_dec: bfloat16 [768, 5, 1536], P(None, None, 'chan'), may hold values from -0.0625 to 0.0625
- targets: bfloat16 [4096, 768], P(('groups', 'seq'), 'chan'), parts along dimension 0, may hold values from -6 to 6
Outputs:
- pred: bfloat16 [4096, 768], P(('groups', 'seq'), 'chan'), parts along dimension 0
- g_enc: float32 [3072, 5, 768], P(('groups', 'seq'), None, 'chan'), parts along dimension 0
- g_dec: float32 [1536, 5, 1536], P(('groups', 'seq'), None, 'chan'), parts along dimension 0
The draws below stay inside these ranges and needn't reach their ends.
There are 2 independent parts, one for each index of `groups`. The reference program is written for one: setup_inputs(seed, part) draws one part's arguments, and reference() takes and returns one part's arrays. A program takes and returns all parts, laid end to end along the dimension named above; an argument that names none is the same for every part. Nothing has to cross between parts.
Inputs may be any that keep to these rules, and one draw needn't show every extreme that they name: `dna_bases`: each entry is one of the four bases.
All inputs are finite; a program needn't handle non-finite values.
Results may differ from the reference program's by a relative error of at most 0.009.
Values may be sent and summed in bfloat16 or wider, within the bound.
A program may use at most 192 MiB of HBM per device.

```python
import math
import jax
import jax.numpy as jnp
from jax import lax

C1 = 768
C2 = 1536
KW = 5
LENGTH = 2048
N_SEQ = 4


def set_ends(drawn, stream_key, least, largest):
    spot = [jax.random.randint(jax.random.fold_in(stream_key, axis), (), 0, length) for axis, length in enumerate(drawn.shape)]
    widest = drawn.shape.index(max(drawn.shape))
    beside = spot[:widest] + [(spot[widest] + 1) % drawn.shape[widest]] + spot[widest + 1:]
    return drawn.at[tuple(spot)].set(least).at[tuple(beside)].set(largest)


def strengthened(values, key, source, target, shards_of, factor):
    def block_of(position):
        return (jnp.arange(values.shape[position]) // (values.shape[position] // shards_of)).reshape((-1,) + (1,) * (values.ndim - 1 - position))

    one_side = jax.random.permutation(key, shards_of)[block_of(target)]
    far = (block_of(target) + shards_of // 2) % shards_of
    return jnp.where((block_of(source) == one_side) | (block_of(source) == far), factor * values, values)


def shard_levels(own_key, shape, shards, least, high):
    def one(position, shards_of):
        steps = jax.random.uniform(jax.random.fold_in(jax.random.fold_in(own_key, 6), position), (shards_of,), jnp.float32, least / len(shards), high / len(shards))
        return jnp.repeat(jnp.exp(steps), shape[position] // shards_of).reshape((-1,) + (1,) * (len(shape) - position - 1))

    factor_of = one(*shards[0])
    for cut in shards[1:]:
        factor_of = factor_of * one(*cut)
    return factor_of


def noise(key, extent, spread, limit, cuts=(), kind=jnp.bfloat16):
    drawn = jax.random.normal(key, extent, jnp.float32) * spread
    if len(cuts) > 0:
        drawn = shard_levels(key, extent, cuts, -0.22, 0.18) * drawn
    return jnp.clip(drawn, min=-limit, max=limit).astype(kind)


def bell_draw_with(stream_key, dims, spread, reach, shards, heavy, kind=jnp.bfloat16):
    values = spread * jax.random.normal(stream_key, dims, jnp.float32)
    if shards:
        values = values * shard_levels(stream_key, dims, shards, -0.22, 0.18)
    return jnp.clip(strengthened(values, jax.random.fold_in(stream_key, 3), *heavy), -reach, reach).astype(kind)


def setup_inputs(seed: int = 0, part: int = 0) -> dict:
    splits = jax.random.split(jax.random.key(seed), 6)
    part_keys = jax.random.split(jax.random.fold_in(splits[5], part), 6)
    dna_bases = set_ends(jax.random.randint(part_keys[0], (LENGTH,), 0, 4), jax.random.fold_in(part_keys[0], 1), 0, 3).astype(jnp.int32)
    w_stem = noise(splits[1], (C1, KW, 4), KW ** -0.5, 2.5, ((0, 4),))
    w_enc = noise(splits[2], (C2, KW, C1), (KW * C1) ** -0.5, 0.09375, ((2, 4),))
    w_dec = noise(splits[3], (C1, KW, C2), (KW * C2) ** -0.5, 0.0625, ((2, 4),))
    targets = bell_draw_with(part_keys[4], (LENGTH, C1), 1.0, 6.0, ((0, 4), (1, 4)), (0, 1, 4, 2.0))
    return dict(dna_bases=dna_bases, w_stem=w_stem, w_enc=w_enc, w_dec=w_dec, targets=targets)


SQRT_TWO_PI = 0.7978845608028654
CUBIC = 0.044715

def gelu_value(value):
    inner = jnp.tanh(SQRT_TWO_PI * (value + CUBIC * value * value * value))
    return 0.5 * value * (1.0 + inner)

def gelu_slope(value):
    inner = jnp.tanh(SQRT_TWO_PI * (value + CUBIC * value * value * value))
    return 0.5 * (1.0 + inner) + 0.5 * value * (1.0 - inner * inner) * SQRT_TWO_PI * (1.0 + 3.0 * CUBIC * value * value)

def pad_rows(array, margin):
    return jnp.pad(array, ((margin, margin), (0, 0)))

def conv_rows(padded, weight):
    row_count = padded.shape[0] - 4
    total = jnp.zeros((row_count, weight.shape[0]), jnp.float32)
    for k in range(KW):
        total = total + jnp.dot(padded[k:k + row_count].astype(jnp.float32), weight[:, k, :].astype(jnp.float32).T)
    return total

def block_grad(cotangent, padded):
    row_count = cotangent.shape[0] // N_SEQ
    width = cotangent.shape[1]

    def one_block(total, index):
        first = index * row_count
        part = lax.dynamic_slice_in_dim(cotangent, first, row_count, 0).astype(jnp.float32)
        window = lax.dynamic_slice_in_dim(padded, first, row_count + 4, 0).astype(jnp.float32)
        pieces = [jnp.dot(part.T, window[k:k + row_count]) for k in range(KW)]
        piece = jnp.stack(pieces, axis=1).astype(jnp.bfloat16)
        return (total + lax.optimization_barrier(piece).astype(jnp.float32), None)
    start_total = jnp.zeros((width, KW, padded.shape[1]), jnp.float32)
    total, _ = lax.scan(one_block, start_total, jnp.arange(N_SEQ, dtype=jnp.int32))
    return total

def reference(dna_bases, w_stem, w_enc, w_dec, targets):
    length = dna_bases.shape[0]
    onehot = (dna_bases[:, None] == jnp.arange(4, dtype=jnp.int32)[None, :]).astype(jnp.bfloat16)
    stem_out = gelu_value(conv_rows(pad_rows(onehot, 2), w_stem)).astype(jnp.bfloat16)
    stem_pad = pad_rows(stem_out, 2)
    enc_pre = conv_rows(stem_pad, w_enc)
    active = gelu_value(enc_pre).astype(jnp.bfloat16).astype(jnp.float32)
    pooled = (0.5 * (active[0::2] + active[1::2])).astype(jnp.bfloat16)
    up_pad = pad_rows(jnp.repeat(pooled, 2, axis=0), 2)
    output = conv_rows(up_pad, w_dec) + stem_out.astype(jnp.float32)
    pred = output.astype(jnp.bfloat16)
    scale = 1.0 / math.sqrt(length)
    slope_out = ((output - targets.astype(jnp.float32)) * scale).astype(jnp.bfloat16)
    g_dec = block_grad(slope_out, up_pad)
    slope_pad = pad_rows(slope_out, 2).astype(jnp.float32)
    up_grad = jnp.zeros((length, w_dec.shape[2]), jnp.float32)
    for k in range(KW):
        up_grad = up_grad + jnp.dot(slope_pad[4 - k:4 - k + length], w_dec[:, k, :].astype(jnp.float32))
    pool_grad = up_grad[0::2] + up_grad[1::2]
    act_grad = 0.5 * jnp.repeat(pool_grad, 2, axis=0)
    pre_grad = (act_grad * gelu_slope(enc_pre)).astype(jnp.bfloat16)
    g_enc = block_grad(pre_grad, stem_pad)
    return (pred, g_enc, g_dec)
```

```python
import functools
import math

import jax
import jax.numpy as jnp
from jax import lax
from jax.experimental import pallas as pl
from jax.experimental.pallas import tpu as pltpu
from jax.sharding import PartitionSpec as P

KW = 5


SQRT_TWO_PI = 0.7978845608028654
CUBIC = 0.044715


def extended(block, sides, width):
    for axis, dim in sides:
        count = lax.axis_size(axis)
        forward = [(i, i + 1) for i in range(count - 1)]
        backward = [(target, source) for source, target in forward]
        low = lax.ppermute(
            lax.slice_in_dim(block, block.shape[dim] - width, None, axis=dim), axis, forward
        )
        high = lax.ppermute(lax.slice_in_dim(block, 0, width, axis=dim), axis, backward)
        block = jnp.concatenate([low, block, high], axis=dim)
    return block


def gelu_value(value):
    inner = jnp.tanh(SQRT_TWO_PI * (value + CUBIC * value * value * value))
    return 0.5 * value * (1.0 + inner)


def gelu_slope(value):
    inner = jnp.tanh(SQRT_TWO_PI * (value + CUBIC * value * value * value))
    return 0.5 * (1.0 + inner) + 0.5 * value * (1.0 - inner * inner) * SQRT_TWO_PI * (
        1.0 + 3.0 * CUBIC * value * value
    )


def rim_cells(block, margin):
    return extended(block, (("seq", 0),), margin)


def channel_sum(partial_value):
    return lax.psum_scatter(partial_value, "chan", scatter_dimension=1, tiled=True)


def channel_gather(block):
    return lax.all_gather(block, "chan", axis=1, tiled=True)


def conv_rows(padded, weight):
    row_count = padded.shape[0] - 4
    total = jnp.zeros((row_count, weight.shape[0]), jnp.float32)
    for k in range(KW):
        total = total + lax.dot_general(
            padded[k : k + row_count],
            weight[:, k, :],
            (((1,), (1,)), ((), ())),
            preferred_element_type=jnp.float32,
        )
    return total


def grad_taps(picked, padded):
    row_count = picked.shape[0]
    pieces = [
        lax.dot_general(
            picked,
            padded[k : k + row_count],
            (((0,), (0,)), ((), ())),
            preferred_element_type=jnp.float32,
        )
        for k in range(KW)
    ]
    return jnp.stack(pieces, axis=1)


def weight_grad(cotangent, padded):
    rounded = grad_taps(cotangent, padded).astype(jnp.bfloat16)
    return lax.psum_scatter(
        lax.optimization_barrier(rounded).astype(jnp.float32),
        "seq",
        scatter_dimension=0,
        tiled=True,
    )


def general_shards(dna_bases, w_stem, w_enc, w_dec, targets):
    row_count = dna_bases.shape[0]
    devices = lax.axis_size("seq")
    length = row_count * devices
    onehot = (dna_bases[:, None] == jnp.arange(4, dtype=jnp.int32)[None, :]).astype(jnp.bfloat16)
    onehot_pad = rim_cells(onehot, 2)
    stem_out = gelu_value(conv_rows(onehot_pad, w_stem)).astype(jnp.bfloat16)
    stem_pad = rim_cells(stem_out, 2)
    enc_pre = channel_sum(conv_rows(stem_pad, w_enc))
    active = gelu_value(enc_pre).astype(jnp.bfloat16).astype(jnp.float32)
    pooled = (0.5 * active.reshape(row_count // 2, 2, -1).sum(axis=1)).astype(jnp.bfloat16)
    pooled_pad = rim_cells(pooled, 1)
    up_pad = jnp.repeat(pooled_pad, 2, axis=0)
    output = channel_sum(conv_rows(up_pad, w_dec)) + stem_out.astype(jnp.float32)
    pred = output.astype(jnp.bfloat16)
    scale = 1.0 / math.sqrt(length)
    slope_out = ((output - targets.astype(jnp.float32)) * scale).astype(jnp.bfloat16)
    slope_all = channel_gather(slope_out)
    g_dec = weight_grad(slope_all, up_pad)
    slope_pad = rim_cells(slope_all, 2)
    up_grad = jnp.zeros((row_count, w_dec.shape[2]), jnp.float32)
    for k in range(KW):
        up_grad = up_grad + jnp.dot(
            slope_pad[4 - k : 4 - k + row_count], w_dec[:, k, :], preferred_element_type=jnp.float32
        )
    pool_grad = up_grad.reshape(row_count // 2, 2, -1).sum(axis=1)
    act_grad = 0.5 * jnp.repeat(pool_grad, 2, axis=0)
    pre_grad = (act_grad * gelu_slope(enc_pre)).astype(jnp.bfloat16)
    pre_all = channel_gather(pre_grad)
    g_enc = weight_grad(pre_all, stem_pad)
    return (pred, g_enc, g_dec)


MESH_ID = pl.DeviceIdType.MESH
BF16 = jnp.bfloat16
EDGE = 16
VMEM_BYTES = 52 * 1024 * 1024


def send(src, dst, send_sem, recv_sem, seq, chan):
    return pltpu.make_async_remote_copy(
        src_ref=src,
        dst_ref=dst,
        send_sem=send_sem,
        recv_sem=recv_sem,
        device_id={"seq": seq, "chan": chan},
        device_id_type=MESH_ID,
    )


def greet(targets):
    barrier = pltpu.get_barrier_semaphore()
    for seq, chan in targets:
        pl.semaphore_signal(
            barrier, inc=1, device_id={"seq": seq, "chan": chan}, device_id_type=MESH_ID
        )
    pl.semaphore_wait(barrier, len(targets))


def whole_group(n, s, c):
    others = []
    for ds in range(n):
        for dc in range(n):
            if ds or dc:
                others.append((lax.rem(s + ds, n), lax.rem(c + dc, n)))
    return others


def bases_kernel(n, own_ref, all_ref, local_sem, send_sem, recv_sem):
    s, c = lax.axis_index("seq"), lax.axis_index("chan")
    peers = [lax.rem(s + d, n) for d in range(1, n)]
    greet([(p, c) for p in peers])
    copies = [
        send(own_ref, all_ref.at[s], send_sem.at[d], recv_sem.at[d], p, c)
        for d, p in enumerate(peers)
    ]
    for copy in copies:
        copy.start()
    mine = pltpu.make_async_copy(own_ref, all_ref.at[s], local_sem)
    mine.start()
    mine.wait()
    for copy in copies:
        copy.wait()


def encoder_kernel(
    n, part_ref, pre_ref, pool_ref, held, wide, edge_lo, edge_hi,
    send_sem, recv_sem, edge_send, edge_recv,
):
    s, c = lax.axis_index("seq"), lax.axis_index("chan")
    rows, width = pre_ref.shape
    half = rows // 2
    peers = [lax.rem(c + d, n) for d in range(1, n)]
    greet([(s, p) for p in peers] + [(lax.rem(s + d, n), c) for d in range(1, n)])
    copies = []
    for d, p in enumerate(peers):
        columns = pl.ds(pl.multiple_of(p * width, 128), width)
        copies.append(
            send(part_ref.at[:, columns], held.at[d], send_sem.at[d], recv_sem.at[d], s, p)
        )
    for copy in copies:
        copy.start()
    own = pl.ds(pl.multiple_of(c * width, 128), width)
    for copy in copies:
        copy.wait_recv()
    step = 64

    @pl.loop(0, rows // step)
    def _(i):
        at = pl.ds(pl.multiple_of(i * step, step), step)
        total = part_ref[at, own].astype(jnp.float32)
        for d in range(n - 1):
            total = total + held[d, at, :].astype(jnp.float32)
        pre_ref[at, :] = total
        active = gelu_value(total).astype(BF16).astype(jnp.float32)
        for j in range(width // 128):
            wide[j, at, :] = active[:, j * 128 : (j + 1) * 128]

    for j in range(width // 128):
        even = wide[j, pl.ds(0, half, stride=2), :]
        odd = wide[j, pl.ds(1, half, stride=2), :]
        pool_ref[EDGE : EDGE + half, j * 128 : (j + 1) * 128] = (0.5 * (even + odd)).astype(BF16)
    up = send(pool_ref.at[pl.ds(half, EDGE)], edge_lo, edge_send.at[0], edge_recv.at[0],
              lax.rem(s + 1, n), c)
    down = send(pool_ref.at[pl.ds(EDGE, EDGE)], edge_hi, edge_send.at[1], edge_recv.at[1],
                lax.rem(s + n - 1, n), c)
    up.start()
    down.start()
    up.wait()
    down.wait()
    pool_ref[0:EDGE, :] = jnp.where(s > 0, edge_lo[...].astype(jnp.float32), 0.0).astype(BF16)
    pool_ref[half + EDGE :, :] = jnp.where(
        s < n - 1, edge_hi[...].astype(jnp.float32), 0.0
    ).astype(BF16)
    for copy in copies:
        copy.wait_send()


def slope_kernel(
    n, scale, part_ref, stem_ref, target_ref, pred_ref, chan_ref, seq_ref, held, slope,
    send_sem, recv_sem, row_send, row_recv, turn_send, turn_recv, lo_send, lo_recv, hi_send, hi_recv,
    local_sem,
):
    s, c = lax.axis_index("seq"), lax.axis_index("chan")
    rows, width = pred_ref.shape
    peers = [lax.rem(c + d, n) for d in range(1, n)]
    greet(whole_group(n, s, c))
    copies = [
        send(part_ref.at[p], held.at[d], send_sem.at[d], recv_sem.at[d], s, p)
        for d, p in enumerate(peers)
    ]
    for copy in copies:
        copy.start()
    for copy in copies:
        copy.wait_recv()
    step = 64

    @pl.loop(0, rows // step)
    def _(i):
        at = pl.ds(pl.multiple_of(i * step, step), step)
        total = part_ref[c, at, :].astype(jnp.float32)
        for d in range(n - 1):
            total = total + held[d, at, :].astype(jnp.float32)
        output = total + stem_ref[at, :].astype(jnp.float32)
        pred_ref[at, :] = output.astype(BF16)
        slope[at, :] = ((output - target_ref[at, :].astype(jnp.float32)) * scale).astype(BF16)

    core = pl.ds(EDGE, rows)
    up, down = lax.rem(s + 1, n), lax.rem(s + n - 1, n)
    row_copies = [
        send(slope, chan_ref.at[c, core], row_send.at[d], row_recv.at[d], s, p)
        for d, p in enumerate(peers)
    ]
    lo_copies, hi_copies = [], []
    for d in range(n):
        p = lax.rem(c + d, n)
        lo_copies.append(
            send(slope.at[pl.ds(rows - EDGE, EDGE)], chan_ref.at[c, pl.ds(0, EDGE)],
                 lo_send.at[d], lo_recv.at[d], up, p)
        )
        hi_copies.append(
            send(slope.at[pl.ds(0, EDGE)], chan_ref.at[c, pl.ds(EDGE + rows, EDGE)],
                 hi_send.at[d], hi_recv.at[d], down, p)
        )
    for copy in row_copies + lo_copies + hi_copies:
        copy.start()
    mine = pltpu.make_async_copy(slope, chan_ref.at[c, core], local_sem.at[0])
    mine.start()
    for j in range(n):
        turned = send(slope, seq_ref.at[s], turn_send.at[j], turn_recv.at[s], c, j)
        itself = jnp.logical_and(s == c, c == j)

        @pl.when(jnp.logical_not(itself))
        def _():
            turned.start()

        @pl.when(itself)
        def _():
            keep = pltpu.make_async_copy(slope, seq_ref.at[s], local_sem.at[1])
            keep.start()
            keep.wait()

    for copy in row_copies + lo_copies + hi_copies:
        copy.wait()
    mine.wait()
    for j in range(n):
        @pl.when(jnp.logical_not(jnp.logical_and(s == c, c == j)))
        def _():
            send(slope, seq_ref.at[s], turn_send.at[j], turn_recv.at[s], c, j).wait_send()

        @pl.when(jnp.logical_not(jnp.logical_and(s == c, s == j)))
        def _():
            send(slope, seq_ref.at[j], turn_send.at[j], turn_recv.at[j], c, j).wait_recv()
    for copy in copies:
        copy.wait_send()
    blank = jnp.zeros((EDGE, width), BF16)

    @pl.when(s == 0)
    def _():
        for j in range(n):
            chan_ref[j, 0:EDGE, :] = blank

    @pl.when(s == n - 1)
    def _():
        for j in range(n):
            chan_ref[j, EDGE + rows :, :] = blank


def turn_kernel(n, own_ref, seq_ref, turn_send, turn_recv, local_sem):
    s, c = lax.axis_index("seq"), lax.axis_index("chan")
    greet(whole_group(n, s, c))
    for j in range(n):
        turned = send(own_ref, seq_ref.at[s], turn_send.at[j], turn_recv.at[s], c, j)
        itself = jnp.logical_and(s == c, c == j)

        @pl.when(jnp.logical_not(itself))
        def _():
            turned.start()

        @pl.when(itself)
        def _():
            keep = pltpu.make_async_copy(own_ref, seq_ref.at[s], local_sem)
            keep.start()
            keep.wait()

    for j in range(n):
        @pl.when(jnp.logical_not(jnp.logical_and(s == c, c == j)))
        def _():
            send(own_ref, seq_ref.at[s], turn_send.at[j], turn_recv.at[s], c, j).wait_send()

        @pl.when(jnp.logical_not(jnp.logical_and(s == c, s == j)))
        def _():
            send(own_ref, seq_ref.at[j], turn_send.at[j], turn_recv.at[j], c, j).wait_recv()


def call(kernel, ident, outs, scratch, *operands):
    vmem = pl.BlockSpec(memory_space=pltpu.VMEM)
    return pl.pallas_call(
        kernel,
        out_shape=outs,
        in_specs=[vmem] * len(operands),
        out_specs=jax.tree.map(lambda _: vmem, outs),
        scratch_shapes=scratch,
        compiler_params=pltpu.CompilerParams(
            collective_id=ident, has_side_effects=True, vmem_limit_bytes=VMEM_BYTES
        ),
    )(*operands)


def dma(count):
    return pltpu.SemaphoreType.DMA((count,))


def all_rows_grad(cotangent, padded):
    count = cotangent.shape[0]
    pieces = [
        lax.dot_general(
            cotangent, padded[k : k + count], (((0,), (0,)), ((), ())),
            preferred_element_type=jnp.float32,
        )
        for k in range(KW)
    ]
    return jnp.stack(pieces, axis=1)


def square_shards(dna_bases, w_stem, w_enc, w_dec, targets):
    rows = dna_bases.shape[0]
    n = lax.axis_size("seq")
    length = rows * n
    s = lax.axis_index("seq")
    c1, c2 = w_stem.shape[0], w_dec.shape[2]
    struct = jax.ShapeDtypeStruct
    bases = call(
        functools.partial(bases_kernel, n), 0, struct((n, rows // 128, 128), jnp.int32),
        [pltpu.SemaphoreType.DMA, dma(n - 1), dma(n - 1)], dna_bases.reshape(rows // 128, 128),
    ).reshape(length)
    bases_pad = jnp.pad(bases, (2, 2), constant_values=-1)
    shifts = jnp.stack([bases_pad[k : k + length] for k in range(KW)])
    onehot = (shifts[:, None, :] == jnp.arange(4, dtype=jnp.int32)[None, :, None]).astype(BF16)
    stem_pre = lax.dot_general(
        onehot.reshape(KW * 4, length), w_stem.reshape(c1, KW * 4), (((0,), (1,)), ((), ())),
        preferred_element_type=jnp.float32,
    )
    stem_all = jnp.pad(gelu_value(stem_pre).astype(BF16), ((2, 2), (0, 0)))
    stem_pad = lax.dynamic_slice_in_dim(stem_all, s * rows, rows + 4, 0)
    part = conv_rows(stem_pad, w_enc).astype(BF16)
    enc_pre, pool_pad = call(
        functools.partial(encoder_kernel, n), 1,
        (struct((rows, c2), jnp.float32), struct((rows // 2 + 2 * EDGE, c2), BF16)),
        [
            pltpu.VMEM((n - 1, rows, c2), BF16),
            pltpu.VMEM((c2 // 128, rows, 128), jnp.float32),
            pltpu.VMEM((EDGE, c2), BF16),
            pltpu.VMEM((EDGE, c2), BF16),
            dma(n - 1), dma(n - 1), dma(2), dma(2),
        ],
        part,
    )
    half = rows // 2
    pool_all = lax.all_gather(pool_pad[EDGE : EDGE + half], "seq", axis=0, tiled=True)
    up_pad = jnp.repeat(pool_pad[EDGE - 1 : EDGE + half + 1], 2, axis=0)
    dec_part = conv_rows(up_pad, w_dec).astype(BF16)
    dec_part = dec_part.reshape(rows, n, c1).transpose(1, 0, 2)
    pred, slope_chan, slope_seq = call(
        functools.partial(slope_kernel, n, 1.0 / math.sqrt(length)), 2,
        (
            struct((rows, c1), BF16),
            struct((n, rows + 2 * EDGE, c1), BF16),
            struct((n, rows, c1), BF16),
        ),
        [
            pltpu.VMEM((n - 1, rows, c1), BF16),
            pltpu.VMEM((rows, c1), BF16),
            dma(n - 1), dma(n - 1), dma(n - 1), dma(n - 1), dma(n), dma(n),
            dma(n), dma(n), dma(n), dma(n), dma(2),
        ],
        dec_part, stem_pad[2 : 2 + rows], targets,
    )
    slope_pad = jnp.concatenate(
        [slope_chan[j, EDGE - 2 : EDGE + rows + 2] for j in range(n)], axis=1
    )
    up_grad = jnp.zeros((rows, c2), jnp.float32)
    for k in range(KW):
        up_grad = up_grad + jnp.dot(
            slope_pad[4 - k : 4 - k + rows], w_dec[:, k, :], preferred_element_type=jnp.float32
        )
    pool_grad = up_grad.reshape(half, 2, -1).sum(axis=1)
    act_grad = 0.5 * jnp.repeat(pool_grad, 2, axis=0)
    pre_grad = (act_grad * gelu_slope(enc_pre)).astype(BF16)
    pre_seq = call(
        functools.partial(turn_kernel, n), 3, struct((n, rows, c2), BF16),
        [dma(n), dma(n), pltpu.SemaphoreType.DMA], pre_grad,
    )
    up_all = jnp.pad(jnp.repeat(pool_all, 2, axis=0), ((2, 2), (0, 0)))
    g_dec = all_rows_grad(slope_seq.reshape(length, c1), up_all)
    g_enc = all_rows_grad(pre_seq.reshape(length, c2), stem_all)
    return (pred, g_enc, g_dec)


def shards(dna_bases, w_stem, w_enc, w_dec, targets):
    args = (dna_bases, w_stem, w_enc, w_dec, targets)
    rows, c1, c2 = dna_bases.shape[0], w_stem.shape[0], w_dec.shape[2]
    n = lax.axis_size("seq")
    square = n == lax.axis_size("chan") and n > 2
    if square and rows % 128 == 0 and c2 % 128 == 0 and c1 % 64 == 0:
        return square_shards(*args)
    return general_shards(*args)


def solution(mesh):
    return jax.shard_map(
        shards,
        mesh=mesh,
        in_specs=(
            P(("groups", "seq")),
            P("chan", None, None),
            P(None, None, "chan"),
            P(None, None, "chan"),
            P(("groups", "seq"), "chan"),
        ),
        out_specs=(
            P(("groups", "seq"), "chan"),
            P(("groups", "seq"), None, "chan"),
            P(("groups", "seq"), None, "chan"),
        ),
        check_vma=False,
    )
```

```python
import functools
import math

import jax
import jax.numpy as jnp
from jax import lax
from jax.experimental import pallas as pl
from jax.experimental.pallas import tpu as pltpu
from jax.sharding import PartitionSpec as P

KW = 5


SQRT_TWO_PI = 0.7978845608028654
CUBIC = 0.044715


def extended(block, sides, width):
    for axis, dim in sides:
        count = lax.axis_size(axis)
        forward = [(i, i + 1) for i in range(count - 1)]
        backward = [(target, source) for source, target in forward]
        low = lax.ppermute(
            lax.slice_in_dim(block, block.shape[dim] - width, None, axis=dim), axis, forward
        )
        high = lax.ppermute(lax.slice_in_dim(block, 0, width, axis=dim), axis, backward)
        block = jnp.concatenate([low, block, high], axis=dim)
    return block


def gelu_value(value):
    inner = jnp.tanh(SQRT_TWO_PI * (value + CUBIC * value * value * value))
    return 0.5 * value * (1.0 + inner)


def gelu_slope(value):
    inner = jnp.tanh(SQRT_TWO_PI * (value + CUBIC * value * value * value))
    return 0.5 * (1.0 + inner) + 0.5 * value * (1.0 - inner * inner) * SQRT_TWO_PI * (
        1.0 + 3.0 * CUBIC * value * value
    )


def rim_cells(block, margin):
    return extended(block, (("seq", 0),), margin)


def channel_sum(partial_value):
    return lax.psum_scatter(partial_value, "chan", scatter_dimension=1, tiled=True)


def channel_gather(block):
    return lax.all_gather(block, "chan", axis=1, tiled=True)


def conv_rows(padded, weight):
    row_count = padded.shape[0] - 4
    total = jnp.zeros((row_count, weight.shape[0]), jnp.float32)
    for k in range(KW):
        total = total + lax.dot_general(
            padded[k : k + row_count],
            weight[:, k, :],
            (((1,), (1,)), ((), ())),
            preferred_element_type=jnp.float32,
        )
    return total


def grad_taps(picked, padded):
    row_count = picked.shape[0]
    pieces = [
        lax.dot_general(
            picked,
            padded[k : k + row_count],
            (((0,), (0,)), ((), ())),
            preferred_element_type=jnp.float32,
        )
        for k in range(KW)
    ]
    return jnp.stack(pieces, axis=1)


def weight_grad(cotangent, padded):
    rounded = grad_taps(cotangent, padded).astype(jnp.bfloat16)
    return lax.psum_scatter(
        lax.optimization_barrier(rounded).astype(jnp.float32),
        "seq",
        scatter_dimension=0,
        tiled=True,
    )


def general_shards(dna_bases, w_stem, w_enc, w_dec, targets):
    row_count = dna_bases.shape[0]
    devices = lax.axis_size("seq")
    length = row_count * devices
    onehot = (dna_bases[:, None] == jnp.arange(4, dtype=jnp.int32)[None, :]).astype(jnp.bfloat16)
    onehot_pad = rim_cells(onehot, 2)
    stem_out = gelu_value(conv_rows(onehot_pad, w_stem)).astype(jnp.bfloat16)
    stem_pad = rim_cells(stem_out, 2)
    enc_pre = channel_sum(conv_rows(stem_pad, w_enc))
    active = gelu_value(enc_pre).astype(jnp.bfloat16).astype(jnp.float32)
    pooled = (0.5 * active.reshape(row_count // 2, 2, -1).sum(axis=1)).astype(jnp.bfloat16)
    pooled_pad = rim_cells(pooled, 1)
    up_pad = jnp.repeat(pooled_pad, 2, axis=0)
    output = channel_sum(conv_rows(up_pad, w_dec)) + stem_out.astype(jnp.float32)
    pred = output.astype(jnp.bfloat16)
    scale = 1.0 / math.sqrt(length)
    slope_out = ((output - targets.astype(jnp.float32)) * scale).astype(jnp.bfloat16)
    slope_all = channel_gather(slope_out)
    g_dec = weight_grad(slope_all, up_pad)
    slope_pad = rim_cells(slope_all, 2)
    up_grad = jnp.zeros((row_count, w_dec.shape[2]), jnp.float32)
    for k in range(KW):
        up_grad = up_grad + jnp.dot(
            slope_pad[4 - k : 4 - k + row_count], w_dec[:, k, :], preferred_element_type=jnp.float32
        )
    pool_grad = up_grad.reshape(row_count // 2, 2, -1).sum(axis=1)
    act_grad = 0.5 * jnp.repeat(pool_grad, 2, axis=0)
    pre_grad = (act_grad * gelu_slope(enc_pre)).astype(jnp.bfloat16)
    pre_all = channel_gather(pre_grad)
    g_enc = weight_grad(pre_all, stem_pad)
    return (pred, g_enc, g_dec)


MESH_ID = pl.DeviceIdType.MESH
BF16 = jnp.bfloat16
EDGE = 16
VMEM_BYTES = 8 * 1024 * 1024


def send(src, dst, send_sem, recv_sem, seq, chan):
    return pltpu.make_async_remote_copy(
        src_ref=src,
        dst_ref=dst,
        send_sem=send_sem,
        recv_sem=recv_sem,
        device_id={"seq": seq, "chan": chan},
        device_id_type=MESH_ID,
    )


def greet(targets):
    barrier = pltpu.get_barrier_semaphore()
    for seq, chan in targets:
        pl.semaphore_signal(
            barrier, inc=1, device_id={"seq": seq, "chan": chan}, device_id_type=MESH_ID
        )
    pl.semaphore_wait(barrier, len(targets))


def whole_group(n, s, c):
    others = []
    for ds in range(n):
        for dc in range(n):
            if ds or dc:
                others.append((lax.rem(s + ds, n), lax.rem(c + dc, n)))
    return others


def bases_kernel(n, own_ref, all_ref, local_sem, send_sem, recv_sem):
    s, c = lax.axis_index("seq"), lax.axis_index("chan")
    peers = [lax.rem(s + d, n) for d in range(1, n)]
    greet([(p, c) for p in peers])
    copies = [
        send(own_ref, all_ref.at[s], send_sem.at[d], recv_sem.at[d], p, c)
        for d, p in enumerate(peers)
    ]
    for copy in copies:
        copy.start()
    mine = pltpu.make_async_copy(own_ref, all_ref.at[s], local_sem)
    mine.start()
    mine.wait()
    for copy in copies:
        copy.wait()


def partners(c):
    mate = c + 1 - 2 * lax.rem(c, 2)
    across = lax.rem(c + 2, 4)
    return mate, across, lax.rem(mate + 2, 4)


class Turn:
    def __init__(self, n, s, c, own, out, sems):
        self.n, self.s, self.c, self.own, self.out = n, s, c, own, out
        self.quarter_send, self.quarter_recv, self.share_send, self.share_recv, self.local = sems
        self.piece = own.shape[0] // n

    def rows(self, index):
        return pl.ds(pl.multiple_of(index * self.piece, self.piece), self.piece)

    def keep(self):
        at = self.rows(self.c)
        return pltpu.make_async_copy(self.own.at[at], self.out.at[self.s, at], self.local)

    def quarter(self, q, slot):
        at = self.rows(q)
        return send(self.own.at[at], self.out.at[self.s, at], self.quarter_send.at[q],
                    self.quarter_recv.at[slot], self.c, q)

    def each(self, action, mine):
        for q in range(self.n):
            itself = jnp.logical_and(self.s == self.c, self.c == q)
            pl.when(jnp.logical_not(itself))(functools.partial(action, q))
        if mine is not None:
            pl.when(self.s == self.c)(mine)

    def start(self):
        self.each(lambda q: self.quarter(q, self.s).start(), lambda: self.keep().start())

    def share(self, slot, kind, part, to):
        at = self.rows(part)
        index = slot * 3 + kind
        return send(self.out.at[slot, at], self.out.at[slot, at], self.share_send.at[index],
                    self.share_recv.at[index], self.s, to)

    def finish(self):
        mate, across, far = partners(self.c)
        slots = [lax.rem(self.s + d, self.n) for d in range(self.n)]
        for d, slot in enumerate(slots):
            if d == 0:
                pl.when(self.s == self.c)(lambda: self.keep().wait())
                pl.when(self.s != self.c)(lambda: self.quarter(self.c, slot).wait_recv())
            else:
                self.quarter(self.c, slot).wait_recv()
            self.share(slot, 1, self.c, across).start()
            self.share(slot, 0, self.c, mate).start()
        for slot in slots:
            self.share(slot, 1, across, across).wait_recv()
            self.share(slot, 2, across, mate).start()
        for slot in slots:
            self.share(slot, 0, mate, mate).wait_recv()
            self.share(slot, 2, far, mate).wait_recv()
        for slot in slots:
            self.share(slot, 0, self.c, mate).wait_send()
            self.share(slot, 1, self.c, across).wait_send()
            self.share(slot, 2, across, mate).wait_send()
        self.each(lambda q: self.quarter(q, self.s).wait_send(), None)


def pair_sum(block, held, pair, s, c, rows, send_sem, recv_sem, finish):
    mate, across, far = partners(c)
    first = send(block(far), held.at[1], send_sem.at[1], recv_sem.at[1], s, mate)
    second = send(block(mate), held.at[0], send_sem.at[0], recv_sem.at[0], s, mate)
    last = send(pair, held.at[2], send_sem.at[2], recv_sem.at[2], s, across)
    first.start()
    second.start()
    step = 64
    first.wait_recv()

    @pl.loop(0, rows // step)
    def _(i):
        at = pl.ds(pl.multiple_of(i * step, step), step)
        pair[at, :] = (
            block(across)[at, :].astype(jnp.float32) + held[1, at, :].astype(jnp.float32)
        ).astype(BF16)

    last.start()
    second.wait_recv()
    last.wait_recv()

    @pl.loop(0, rows // step)
    def _(i):
        at = pl.ds(pl.multiple_of(i * step, step), step)
        total = block(c)[at, :].astype(jnp.float32) + held[0, at, :].astype(jnp.float32)
        finish(at, total + held[2, at, :].astype(jnp.float32))

    return [first, second, last]


def encoder_kernel(
    n, part_ref, pre_ref, pool_ref, held, pair, wide, edge_lo, edge_hi,
    send_sem, recv_sem, edge_send, edge_recv,
):
    s, c = lax.axis_index("seq"), lax.axis_index("chan")
    rows, width = pre_ref.shape
    half = rows // 2
    greet(
        [(s, lax.rem(c + d, n)) for d in range(1, n)]
        + [(lax.rem(s + d, n), c) for d in range(1, n)]
    )

    def block(j):
        return part_ref.at[:, pl.ds(pl.multiple_of(j * width, 128), width)]

    def finish(at, total):
        pre_ref[at, :] = total
        active = gelu_value(total).astype(BF16).astype(jnp.float32)
        for j in range(width // 128):
            wide[j, at, :] = active[:, j * 128 : (j + 1) * 128]

    copies = pair_sum(block, held, pair, s, c, rows, send_sem, recv_sem, finish)
    for j in range(width // 128):
        even = wide[j, pl.ds(0, half, stride=2), :]
        odd = wide[j, pl.ds(1, half, stride=2), :]
        pool_ref[EDGE : EDGE + half, j * 128 : (j + 1) * 128] = (0.5 * (even + odd)).astype(BF16)
    up = send(pool_ref.at[pl.ds(half, EDGE)], edge_lo, edge_send.at[0], edge_recv.at[0],
              lax.rem(s + 1, n), c)
    down = send(pool_ref.at[pl.ds(EDGE, EDGE)], edge_hi, edge_send.at[1], edge_recv.at[1],
                lax.rem(s + n - 1, n), c)
    up.start()
    down.start()
    up.wait()
    down.wait()
    pool_ref[0:EDGE, :] = jnp.where(s > 0, edge_lo[...].astype(jnp.float32), 0.0).astype(BF16)
    pool_ref[half + EDGE :, :] = jnp.where(
        s < n - 1, edge_hi[...].astype(jnp.float32), 0.0
    ).astype(BF16)
    for copy in copies:
        copy.wait_send()


def slope_kernel(
    n, scale, part_ref, stem_ref, target_ref, pool_ref, pred_ref, chan_ref, seq_ref, all_ref,
    held, pair, slope, send_sem, recv_sem, row_send, row_recv, lo_send, lo_recv, hi_send, hi_recv,
    pool_send, pool_recv, local_sem, *turn_sems,
):
    s, c = lax.axis_index("seq"), lax.axis_index("chan")
    rows, width = pred_ref.shape
    mate, across, far = partners(c)
    greet(whole_group(n, s, c))
    pool_own = pool_ref.at[pl.ds(EDGE, rows // 2)]

    def finish(at, total):
        output = total + stem_ref[at, :].astype(jnp.float32)
        pred_ref[at, :] = output.astype(BF16)
        slope[at, :] = ((output - target_ref[at, :].astype(jnp.float32)) * scale).astype(BF16)

    pool_copies = [
        send(pool_own, all_ref.at[s], pool_send.at[d], pool_recv.at[d], lax.rem(s + 1 + d, n), c)
        for d in range(n - 1)
    ]
    pool_mine = pltpu.make_async_copy(pool_own, all_ref.at[s], local_sem.at[1])
    for copy in pool_copies:
        copy.start()
    pool_mine.start()
    copies = pair_sum(
        lambda j: part_ref.at[j], held, pair, s, c, rows, send_sem, recv_sem, finish
    )
    core = pl.ds(EDGE, rows)
    up, down = lax.rem(s + 1, n), lax.rem(s + n - 1, n)

    def row_copy(index, src, owner, to):
        return send(src, chan_ref.at[owner, core], row_send.at[index], row_recv.at[index], s, to)

    to_across = row_copy(1, slope, c, across)
    to_mate = row_copy(0, slope, c, mate)
    relay = row_copy(2, chan_ref.at[across, core], across, mate)
    lo_copies, hi_copies = [], []
    for d in range(n):
        p = lax.rem(c + d, n)
        lo_copies.append(
            send(slope.at[pl.ds(rows - EDGE, EDGE)], chan_ref.at[c, pl.ds(0, EDGE)],
                 lo_send.at[d], lo_recv.at[d], up, p)
        )
        hi_copies.append(
            send(slope.at[pl.ds(0, EDGE)], chan_ref.at[c, pl.ds(EDGE + rows, EDGE)],
                 hi_send.at[d], hi_recv.at[d], down, p)
        )
    for copy in [to_across, to_mate] + lo_copies + hi_copies:
        copy.start()
    mine = pltpu.make_async_copy(slope, chan_ref.at[c, core], local_sem.at[0])
    mine.start()
    turn = Turn(n, s, c, slope, seq_ref, turn_sems)
    turn.start()
    to_across.wait_recv()
    relay.start()
    turn.finish()
    to_across.wait_send()
    to_mate.wait()
    relay.wait()
    for copy in lo_copies + hi_copies + pool_copies:
        copy.wait()
    mine.wait()
    pool_mine.wait()
    for copy in copies:
        copy.wait_send()
    blank = jnp.zeros((EDGE, width), BF16)

    @pl.when(s == 0)
    def _():
        for j in range(n):
            chan_ref[j, 0:EDGE, :] = blank

    @pl.when(s == n - 1)
    def _():
        for j in range(n):
            chan_ref[j, EDGE + rows :, :] = blank


def turn_kernel(n, own_ref, seq_ref, *turn_sems):
    s, c = lax.axis_index("seq"), lax.axis_index("chan")
    greet(whole_group(n, s, c))
    turn = Turn(n, s, c, own_ref, seq_ref, turn_sems)
    turn.start()
    turn.finish()


def turn_scratch(n):
    return [dma(n), dma(n), dma(3 * n), dma(3 * n), pltpu.SemaphoreType.DMA]


def call(kernel, ident, outs, scratch, *operands):
    vmem = pl.BlockSpec(memory_space=pltpu.VMEM)
    return pl.pallas_call(
        kernel,
        out_shape=outs,
        in_specs=[vmem] * len(operands),
        out_specs=jax.tree.map(lambda _: vmem, outs),
        scratch_shapes=scratch,
        compiler_params=pltpu.CompilerParams(
            collective_id=ident, has_side_effects=True, vmem_limit_bytes=VMEM_BYTES
        ),
    )(*operands)


def dma(count):
    return pltpu.SemaphoreType.DMA((count,))


def all_rows_grad(cotangent, padded):
    count = cotangent.shape[0]
    pieces = [
        lax.dot_general(
            cotangent, padded[k : k + count], (((0,), (0,)), ((), ())),
            preferred_element_type=jnp.float32,
        )
        for k in range(KW)
    ]
    return jnp.stack(pieces, axis=1)


def square_shards(dna_bases, w_stem, w_enc, w_dec, targets):
    rows = dna_bases.shape[0]
    n = lax.axis_size("seq")
    length = rows * n
    s = lax.axis_index("seq")
    c1, c2 = w_stem.shape[0], w_dec.shape[2]
    struct = jax.ShapeDtypeStruct
    bases = call(
        functools.partial(bases_kernel, n), 0, struct((n, rows // 128, 128), jnp.int32),
        [pltpu.SemaphoreType.DMA, dma(n - 1), dma(n - 1)], dna_bases.reshape(rows // 128, 128),
    ).reshape(length)
    bases_pad = jnp.pad(bases, (2, 2), constant_values=-1)
    shifts = jnp.stack([bases_pad[k : k + length] for k in range(KW)])
    onehot = (shifts[:, None, :] == jnp.arange(4, dtype=jnp.int32)[None, :, None]).astype(BF16)
    stem_pre = lax.dot_general(
        onehot.reshape(KW * 4, length), w_stem.reshape(c1, KW * 4), (((0,), (1,)), ((), ())),
        preferred_element_type=jnp.float32,
    )
    stem_all = jnp.pad(gelu_value(stem_pre).astype(BF16), ((2, 2), (0, 0)))
    stem_pad = lax.dynamic_slice_in_dim(stem_all, s * rows, rows + 4, 0)
    part = conv_rows(stem_pad, w_enc).astype(BF16)
    enc_pre, pool_pad = call(
        functools.partial(encoder_kernel, n), 1,
        (struct((rows, c2), jnp.float32), struct((rows // 2 + 2 * EDGE, c2), BF16)),
        [
            pltpu.VMEM((n - 1, rows, c2), BF16),
            pltpu.VMEM((rows, c2), BF16),
            pltpu.VMEM((c2 // 128, rows, 128), jnp.float32),
            pltpu.VMEM((EDGE, c2), BF16),
            pltpu.VMEM((EDGE, c2), BF16),
            dma(n - 1), dma(n - 1), dma(2), dma(2),
        ],
        part,
    )
    half = rows // 2
    up_pad = jnp.repeat(pool_pad[EDGE - 1 : EDGE + half + 1], 2, axis=0)
    dec_part = conv_rows(up_pad, w_dec).astype(BF16)
    dec_part = dec_part.reshape(rows, n, c1).transpose(1, 0, 2)
    pred, slope_chan, slope_seq, pool_all = call(
        functools.partial(slope_kernel, n, 1.0 / math.sqrt(length)), 2,
        (
            struct((rows, c1), BF16),
            struct((n, rows + 2 * EDGE, c1), BF16),
            struct((n, rows, c1), BF16),
            struct((n, half, c2), BF16),
        ),
        [
            pltpu.VMEM((n - 1, rows, c1), BF16),
            pltpu.VMEM((rows, c1), BF16),
            pltpu.VMEM((rows, c1), BF16),
            dma(3), dma(3), dma(3), dma(3), dma(n), dma(n), dma(n), dma(n),
            dma(n - 1), dma(n - 1), dma(2),
            *turn_scratch(n),
        ],
        dec_part, stem_pad[2 : 2 + rows], targets, pool_pad,
    )
    slope_pad = jnp.concatenate(
        [slope_chan[j, EDGE - 2 : EDGE + rows + 2] for j in range(n)], axis=1
    )
    up_grad = jnp.zeros((rows, c2), jnp.float32)
    for k in range(KW):
        up_grad = up_grad + jnp.dot(
            slope_pad[4 - k : 4 - k + rows], w_dec[:, k, :], preferred_element_type=jnp.float32
        )
    pool_grad = up_grad.reshape(half, 2, -1).sum(axis=1)
    act_grad = 0.5 * jnp.repeat(pool_grad, 2, axis=0)
    pre_grad = (act_grad * gelu_slope(enc_pre)).astype(BF16)
    pre_seq = call(
        functools.partial(turn_kernel, n), 3, struct((n, rows, c2), BF16),
        turn_scratch(n), pre_grad,
    )
    up_all = jnp.pad(jnp.repeat(pool_all.reshape(length // 2, c2), 2, axis=0), ((2, 2), (0, 0)))
    g_dec = all_rows_grad(slope_seq.reshape(length, c1), up_all)
    g_enc = all_rows_grad(pre_seq.reshape(length, c2), stem_all)
    return (pred, g_enc, g_dec)


def shards(dna_bases, w_stem, w_enc, w_dec, targets):
    args = (dna_bases, w_stem, w_enc, w_dec, targets)
    rows, c1, c2 = dna_bases.shape[0], w_stem.shape[0], w_dec.shape[2]
    n = lax.axis_size("seq")
    square = n == 4 and lax.axis_size("chan") == 4
    if square and rows % 128 == 0 and c2 % 128 == 0 and c1 % 64 == 0:
        return square_shards(*args)
    return general_shards(*args)


def solution(mesh):
    return jax.shard_map(
        shards,
        mesh=mesh,
        in_specs=(
            P(("groups", "seq")),
            P("chan", None, None),
            P(None, None, "chan"),
            P(None, None, "chan"),
            P(("groups", "seq"), "chan"),
        ),
        out_specs=(
            P(("groups", "seq"), "chan"),
            P(("groups", "seq"), None, "chan"),
            P(("groups", "seq"), None, "chan"),
        ),
        check_vma=False,
    )
```

```python
import functools
import math

import jax
import jax.numpy as jnp
from jax import lax
from jax.experimental import pallas as pl
from jax.experimental.pallas import tpu as pltpu
from jax.sharding import PartitionSpec as P

KW = 5


SQRT_TWO_PI = 0.7978845608028654
CUBIC = 0.044715


def extended(block, sides, width):
    for axis, dim in sides:
        count = lax.axis_size(axis)
        forward = [(i, i + 1) for i in range(count - 1)]
        backward = [(target, source) for source, target in forward]
        low = lax.ppermute(
            lax.slice_in_dim(block, block.shape[dim] - width, None, axis=dim), axis, forward
        )
        high = lax.ppermute(lax.slice_in_dim(block, 0, width, axis=dim), axis, backward)
        block = jnp.concatenate([low, block, high], axis=dim)
    return block


def gelu_value(value):
    inner = jnp.tanh(SQRT_TWO_PI * (value + CUBIC * value * value * value))
    return 0.5 * value * (1.0 + inner)


def gelu_slope(value):
    inner = jnp.tanh(SQRT_TWO_PI * (value + CUBIC * value * value * value))
    return 0.5 * (1.0 + inner) + 0.5 * value * (1.0 - inner * inner) * SQRT_TWO_PI * (
        1.0 + 3.0 * CUBIC * value * value
    )


def rim_cells(block, margin):
    return extended(block, (("seq", 0),), margin)


def channel_sum(partial_value):
    return lax.psum_scatter(partial_value, "chan", scatter_dimension=1, tiled=True)


def channel_gather(block):
    return lax.all_gather(block, "chan", axis=1, tiled=True)


def conv_rows(padded, weight):
    row_count = padded.shape[0] - 4
    total = jnp.zeros((row_count, weight.shape[0]), jnp.float32)
    for k in range(KW):
        total = total + lax.dot_general(
            padded[k : k + row_count],
            weight[:, k, :],
            (((1,), (1,)), ((), ())),
            preferred_element_type=jnp.float32,
        )
    return total


def grad_taps(picked, padded):
    row_count = picked.shape[0]
    pieces = [
        lax.dot_general(
            picked,
            padded[k : k + row_count],
            (((0,), (0,)), ((), ())),
            preferred_element_type=jnp.float32,
        )
        for k in range(KW)
    ]
    return jnp.stack(pieces, axis=1)


def weight_grad(cotangent, padded):
    rounded = grad_taps(cotangent, padded).astype(jnp.bfloat16)
    return lax.psum_scatter(
        lax.optimization_barrier(rounded).astype(jnp.float32),
        "seq",
        scatter_dimension=0,
        tiled=True,
    )


def general_shards(dna_bases, w_stem, w_enc, w_dec, targets):
    row_count = dna_bases.shape[0]
    devices = lax.axis_size("seq")
    length = row_count * devices
    onehot = (dna_bases[:, None] == jnp.arange(4, dtype=jnp.int32)[None, :]).astype(jnp.bfloat16)
    onehot_pad = rim_cells(onehot, 2)
    stem_out = gelu_value(conv_rows(onehot_pad, w_stem)).astype(jnp.bfloat16)
    stem_pad = rim_cells(stem_out, 2)
    enc_pre = channel_sum(conv_rows(stem_pad, w_enc))
    active = gelu_value(enc_pre).astype(jnp.bfloat16).astype(jnp.float32)
    pooled = (0.5 * active.reshape(row_count // 2, 2, -1).sum(axis=1)).astype(jnp.bfloat16)
    pooled_pad = rim_cells(pooled, 1)
    up_pad = jnp.repeat(pooled_pad, 2, axis=0)
    output = channel_sum(conv_rows(up_pad, w_dec)) + stem_out.astype(jnp.float32)
    pred = output.astype(jnp.bfloat16)
    scale = 1.0 / math.sqrt(length)
    slope_out = ((output - targets.astype(jnp.float32)) * scale).astype(jnp.bfloat16)
    slope_all = channel_gather(slope_out)
    g_dec = weight_grad(slope_all, up_pad)
    slope_pad = rim_cells(slope_all, 2)
    up_grad = jnp.zeros((row_count, w_dec.shape[2]), jnp.float32)
    for k in range(KW):
        up_grad = up_grad + jnp.dot(
            slope_pad[4 - k : 4 - k + row_count], w_dec[:, k, :], preferred_element_type=jnp.float32
        )
    pool_grad = up_grad.reshape(row_count // 2, 2, -1).sum(axis=1)
    act_grad = 0.5 * jnp.repeat(pool_grad, 2, axis=0)
    pre_grad = (act_grad * gelu_slope(enc_pre)).astype(jnp.bfloat16)
    pre_all = channel_gather(pre_grad)
    g_enc = weight_grad(pre_all, stem_pad)
    return (pred, g_enc, g_dec)


MESH_ID = pl.DeviceIdType.MESH
BF16 = jnp.bfloat16
EDGE = 16
VMEM_BYTES = 8 * 1024 * 1024


def send(src, dst, send_sem, recv_sem, seq, chan):
    return pltpu.make_async_remote_copy(
        src_ref=src,
        dst_ref=dst,
        send_sem=send_sem,
        recv_sem=recv_sem,
        device_id={"seq": seq, "chan": chan},
        device_id_type=MESH_ID,
    )


def greet(targets):
    barrier = pltpu.get_barrier_semaphore()
    for seq, chan in targets:
        pl.semaphore_signal(
            barrier, inc=1, device_id={"seq": seq, "chan": chan}, device_id_type=MESH_ID
        )
    pl.semaphore_wait(barrier, len(targets))


def whole_group(n, s, c):
    others = []
    for ds in range(n):
        for dc in range(n):
            if ds or dc:
                others.append((lax.rem(s + ds, n), lax.rem(c + dc, n)))
    return others


def bases_kernel(n, own_ref, all_ref, local_sem, send_sem, recv_sem):
    s, c = lax.axis_index("seq"), lax.axis_index("chan")
    peers = [lax.rem(s + d, n) for d in range(1, n)]
    greet([(p, c) for p in peers])
    copies = [
        send(own_ref, all_ref.at[s], send_sem.at[d], recv_sem.at[d], p, c)
        for d, p in enumerate(peers)
    ]
    for copy in copies:
        copy.start()
    mine = pltpu.make_async_copy(own_ref, all_ref.at[s], local_sem)
    mine.start()
    mine.wait()
    for copy in copies:
        copy.wait()


def partners(c):
    mate = c + 1 - 2 * lax.rem(c, 2)
    across = lax.rem(c + 2, 4)
    return mate, across, lax.rem(mate + 2, 4)


class Turn:
    def __init__(self, n, s, c, own, out, sems):
        self.n, self.s, self.c, self.own, self.out = n, s, c, own, out
        self.quarter_send, self.quarter_recv, self.share_send, self.share_recv, self.local = sems
        self.piece = own.shape[0] // n

    def rows(self, index):
        return pl.ds(pl.multiple_of(index * self.piece, self.piece), self.piece)

    def keep(self):
        at = self.rows(self.c)
        return pltpu.make_async_copy(self.own.at[at], self.out.at[self.s, at], self.local)

    def quarter(self, q, slot):
        at = self.rows(q)
        return send(self.own.at[at], self.out.at[self.s, at], self.quarter_send.at[q],
                    self.quarter_recv.at[slot], self.c, q)

    def each(self, action, mine, before=None):
        for q in range(self.n):
            if before is not None:
                before(q * self.piece)
            itself = jnp.logical_and(self.s == self.c, self.c == q)
            pl.when(jnp.logical_not(itself))(functools.partial(action, q))
        if mine is not None:
            pl.when(self.s == self.c)(mine)

    def start(self, before=None):
        self.each(
            lambda q: self.quarter(q, self.s).start(), lambda: self.keep().start(), before
        )

    def share(self, slot, kind, part, to):
        at = self.rows(part)
        index = slot * 3 + kind
        return send(self.out.at[slot, at], self.out.at[slot, at], self.share_send.at[index],
                    self.share_recv.at[index], self.s, to)

    def finish(self, between=None):
        mate, across, far = partners(self.c)
        slots = [lax.rem(self.s + d, self.n) for d in range(self.n)]
        for d, slot in enumerate(slots):
            if d == 0:
                pl.when(self.s == self.c)(lambda: self.keep().wait())
                pl.when(self.s != self.c)(lambda: self.quarter(self.c, slot).wait_recv())
            else:
                self.quarter(self.c, slot).wait_recv()
            self.share(slot, 1, self.c, across).start()
            self.share(slot, 0, self.c, mate).start()
        if between is not None:
            between()
        for slot in slots:
            self.share(slot, 1, across, across).wait_recv()
            self.share(slot, 2, across, mate).start()
        for slot in slots:
            self.share(slot, 0, mate, mate).wait_recv()
            self.share(slot, 2, far, mate).wait_recv()
        for slot in slots:
            self.share(slot, 0, self.c, mate).wait_send()
            self.share(slot, 1, self.c, across).wait_send()
            self.share(slot, 2, across, mate).wait_send()
        self.each(lambda q: self.quarter(q, self.s).wait_send(), None)


def pair_sum(block, held, pair, s, c, rows, send_sem, recv_sem, finish):
    mate, across, far = partners(c)
    first = send(block(far), held.at[1], send_sem.at[1], recv_sem.at[1], s, mate)
    second = send(block(mate), held.at[0], send_sem.at[0], recv_sem.at[0], s, mate)
    last = send(pair, held.at[2], send_sem.at[2], recv_sem.at[2], s, across)
    first.start()
    second.start()
    step = 64
    first.wait_recv()

    @pl.loop(0, rows // step)
    def _(i):
        at = pl.ds(pl.multiple_of(i * step, step), step)
        pair[at, :] = (
            block(across)[at, :].astype(jnp.float32) + held[1, at, :].astype(jnp.float32)
        ).astype(BF16)

    last.start()
    second.wait_recv()
    last.wait_recv()

    @pl.loop(0, rows // step)
    def _(i):
        at = pl.ds(pl.multiple_of(i * step, step), step)
        total = block(c)[at, :].astype(jnp.float32) + held[0, at, :].astype(jnp.float32)
        finish(at, total + held[2, at, :].astype(jnp.float32))

    return [first, second, last]


def pair_add(value):
    count = value.shape[0]
    row = lax.broadcasted_iota(jnp.int32, value.shape, 0)
    other = jnp.where(
        lax.rem(row, 2) == 0, pltpu.roll(value, count - 1, 0), pltpu.roll(value, 1, 0)
    )
    return value + other


def encoder_kernel(
    n, part_ref, pre_ref, up_ref, pool_ref, held, pair, wide,
    send_sem, recv_sem, edge_send, edge_recv,
):
    s, c = lax.axis_index("seq"), lax.axis_index("chan")
    rows, width = pre_ref.shape
    half = rows // 2
    greet(
        [(s, lax.rem(c + d, n)) for d in range(1, n)]
        + [(lax.rem(s + d, n), c) for d in range(1, n)]
    )

    def block(j):
        return part_ref.at[:, pl.ds(pl.multiple_of(j * width, 128), width)]

    def finish(at, total):
        pre_ref[at, :] = total
        active = gelu_value(total).astype(BF16).astype(jnp.float32)
        pooled = (0.5 * pair_add(active)).astype(BF16)
        up_ref[pl.ds(pl.multiple_of(at.start + EDGE, EDGE), at.size), :] = pooled
        for j in range(width // 128):
            wide[j, at, :] = pooled[:, j * 128 : (j + 1) * 128].astype(jnp.float32)

    copies = pair_sum(block, held, pair, s, c, rows, send_sem, recv_sem, finish)
    up = send(up_ref.at[pl.ds(rows, EDGE)], up_ref.at[pl.ds(0, EDGE)], edge_send.at[0],
              edge_recv.at[0], lax.rem(s + 1, n), c)
    down = send(up_ref.at[pl.ds(EDGE, EDGE)], up_ref.at[pl.ds(rows + EDGE, EDGE)],
                edge_send.at[1], edge_recv.at[1], lax.rem(s + n - 1, n), c)
    up.start()
    down.start()
    for j in range(width // 128):
        pool_ref[:, j * 128 : (j + 1) * 128] = wide[j, pl.ds(0, half, stride=2), :].astype(BF16)
    up.wait()
    down.wait()
    blank = jnp.zeros((EDGE, width), BF16)

    @pl.when(s == 0)
    def _():
        up_ref[0:EDGE, :] = blank

    @pl.when(s == n - 1)
    def _():
        up_ref[rows + EDGE :, :] = blank

    for copy in copies:
        copy.wait_send()


class PoolRelay:
    def __init__(self, n, s, c, own, out, right_send, left_send, recv, local):
        self.n, self.s, self.c, self.own, self.out = n, s, c, own, out
        self.right_send, self.left_send, self.recv = right_send, left_send, recv
        self.mine = pltpu.make_async_copy(own, out.at[s], local)

    def hop(self, src, slot, step):
        sems = self.right_send if step > 0 else self.left_send
        return send(src, self.out.at[slot], sems.at[slot], self.recv.at[slot], self.s + step, self.c)

    def start(self):
        pl.when(self.s < self.n - 1)(lambda: self.hop(self.own, self.s, 1).start())
        pl.when(self.s > 0)(lambda: self.hop(self.own, self.s, -1).start())
        self.mine.start()

    def arrive(self, d):
        low, high = self.s - d, self.s + d

        @pl.when(low >= 0)
        def _():
            self.hop(self.out.at[low], low, 1).wait_recv()
            pl.when(self.s < self.n - 1)(lambda: self.hop(self.out.at[low], low, 1).start())

        @pl.when(high < self.n)
        def _():
            self.hop(self.out.at[high], high, -1).wait_recv()
            pl.when(self.s > 0)(lambda: self.hop(self.out.at[high], high, -1).start())

    def end(self):
        self.mine.wait()
        for slot in range(self.n):
            pl.when(jnp.logical_and(slot <= self.s, self.s < self.n - 1))(
                lambda: self.hop(self.own, slot, 1).wait_send()
            )
            pl.when(jnp.logical_and(slot >= self.s, self.s > 0))(
                lambda: self.hop(self.own, slot, -1).wait_send()
            )


def slope_kernel(
    n, scale, part_ref, stem_ref, target_ref, pool_ref, pred_ref, chan_ref, seq_ref, up_ref,
    held, pair, slope, all_ref, wide, send_sem, recv_sem, row_send, row_recv, lo_send, lo_recv, hi_send, hi_recv,
    right_send, left_send, pool_recv, local_sem, *turn_sems,
):
    s, c = lax.axis_index("seq"), lax.axis_index("chan")
    rows, width = pred_ref.shape
    mate, across, far = partners(c)
    greet(whole_group(n, s, c))
    half, up_width = pool_ref.shape
    pools = PoolRelay(
        n, s, c, pool_ref, all_ref, right_send, left_send, pool_recv, local_sem.at[1]
    )

    def finish(at, total):
        output = total + stem_ref[at, :].astype(jnp.float32)
        pred_ref[at, :] = output.astype(BF16)
        slope[at, :] = ((output - target_ref[at, :].astype(jnp.float32)) * scale).astype(BF16)

    pools.start()
    copies = pair_sum(
        lambda j: part_ref.at[j], held, pair, s, c, rows, send_sem, recv_sem, finish
    )
    pools.arrive(1)
    core = pl.ds(EDGE, rows)
    up, down = lax.rem(s + 1, n), lax.rem(s + n - 1, n)

    def row_copy(index, src, owner, to):
        return send(src, chan_ref.at[owner, core], row_send.at[index], row_recv.at[index], s, to)

    to_across = row_copy(1, slope, c, across)
    to_mate = row_copy(0, slope, c, mate)
    relay = row_copy(2, chan_ref.at[across, core], across, mate)
    lo_copies, hi_copies = [], []
    for d in range(n):
        p = lax.rem(c + d, n)
        lo_copies.append(
            send(slope.at[pl.ds(rows - EDGE, EDGE)], chan_ref.at[c, pl.ds(0, EDGE)],
                 lo_send.at[d], lo_recv.at[d], up, p)
        )
        hi_copies.append(
            send(slope.at[pl.ds(0, EDGE)], chan_ref.at[c, pl.ds(EDGE + rows, EDGE)],
                 hi_send.at[d], hi_recv.at[d], down, p)
        )
    for copy in [to_across, to_mate] + lo_copies + hi_copies:
        copy.start()
    mine = pltpu.make_async_copy(slope, chan_ref.at[c, core], local_sem.at[0])
    mine.start()
    turn = Turn(n, s, c, slope, seq_ref, turn_sems)
    turn.start()
    pools.arrive(2)
    to_across.wait_recv()
    relay.start()

    def upsample():
        pools.arrive(3)
        pools.end()

        @pl.loop(0, n)
        def _(slot):
            for j in range(up_width // 128):
                lanes = slice(j * 128, (j + 1) * 128)
                value = all_ref[slot, :, lanes].astype(jnp.float32)
                wide[j, pl.ds(0, half, stride=2), :] = value
                wide[j, pl.ds(1, half, stride=2), :] = value
                up_ref[slot, :, lanes] = wide[j].astype(BF16)

    turn.finish(upsample)
    to_across.wait_send()
    to_mate.wait()
    relay.wait()
    for copy in lo_copies + hi_copies:
        copy.wait()
    mine.wait()
    for copy in copies:
        copy.wait_send()
    blank = jnp.zeros((EDGE, width), BF16)

    @pl.when(s == 0)
    def _():
        for j in range(n):
            chan_ref[j, 0:EDGE, :] = blank

    @pl.when(s == n - 1)
    def _():
        for j in range(n):
            chan_ref[j, EDGE + rows :, :] = blank


def turn_kernel(n, grad_ref, pre_ref, seq_ref, own, *turn_sems):
    s, c = lax.axis_index("seq"), lax.axis_index("chan")
    greet(whole_group(n, s, c))
    turn = Turn(n, s, c, own, seq_ref, turn_sems)
    step = 64
    pieces = turn.piece // step

    def slope_rows(first):
        @pl.loop(0, pieces)
        def _(i):
            at = pl.ds(pl.multiple_of(first + i * step, step), step)
            grad = 0.5 * pair_add(grad_ref[at, :])
            own[at, :] = (grad * gelu_slope(pre_ref[at, :])).astype(BF16)

    turn.start(slope_rows)
    turn.finish()


def turn_scratch(n):
    return [dma(n), dma(n), dma(3 * n), dma(3 * n), pltpu.SemaphoreType.DMA]


def call(kernel, ident, outs, scratch, *operands):
    vmem = pl.BlockSpec(memory_space=pltpu.VMEM)
    return pl.pallas_call(
        kernel,
        out_shape=outs,
        in_specs=[vmem] * len(operands),
        out_specs=jax.tree.map(lambda _: vmem, outs),
        scratch_shapes=scratch,
        compiler_params=pltpu.CompilerParams(
            collective_id=ident, has_side_effects=True, vmem_limit_bytes=VMEM_BYTES
        ),
    )(*operands)


def dma(count):
    return pltpu.SemaphoreType.DMA((count,))


def windows(padded):
    count = padded.shape[0] - 4
    return jnp.stack([padded[k : k + count] for k in range(KW)], axis=0)


def conv_stack(padded, weight):
    return lax.dot_general(
        windows(padded), weight, (((0, 2), (1, 2)), ((), ())), preferred_element_type=jnp.float32
    )


def all_rows_grad(cotangent, padded):
    count = cotangent.shape[0]
    pieces = [
        lax.dot_general(
            cotangent, padded[k : k + count], (((0,), (0,)), ((), ())),
            preferred_element_type=jnp.float32,
        )
        for k in range(KW)
    ]
    return jnp.stack(pieces, axis=1)


def square_shards(dna_bases, w_stem, w_enc, w_dec, targets):
    rows = dna_bases.shape[0]
    n = lax.axis_size("seq")
    length = rows * n
    s = lax.axis_index("seq")
    c1, c2 = w_stem.shape[0], w_dec.shape[2]
    struct = jax.ShapeDtypeStruct
    bases = call(
        functools.partial(bases_kernel, n), 0, struct((n, rows // 128, 128), jnp.int32),
        [pltpu.SemaphoreType.DMA, dma(n - 1), dma(n - 1)], dna_bases.reshape(rows // 128, 128),
    ).reshape(length)
    bases_pad = jnp.pad(bases, (2, 2), constant_values=-1)
    shifts = jnp.stack([bases_pad[k : k + length] for k in range(KW)])
    onehot = (shifts[:, None, :] == jnp.arange(4, dtype=jnp.int32)[None, :, None]).astype(BF16)
    stem_pre = lax.dot_general(
        onehot.reshape(KW * 4, length), w_stem.reshape(c1, KW * 4), (((0,), (1,)), ((), ())),
        preferred_element_type=jnp.float32,
    )
    stem_all = jnp.pad(gelu_value(stem_pre).astype(BF16), ((2, 2), (0, 0)))
    stem_pad = lax.dynamic_slice_in_dim(stem_all, s * rows, rows + 4, 0)
    part = conv_stack(stem_pad, w_enc).astype(BF16)
    half = rows // 2
    enc_pre, up_own, pool = call(
        functools.partial(encoder_kernel, n), 1,
        (
            struct((rows, c2), jnp.float32),
            struct((rows + 2 * EDGE, c2), BF16),
            struct((half, c2), BF16),
        ),
        [
            pltpu.VMEM((n - 1, rows, c2), BF16),
            pltpu.VMEM((rows, c2), BF16),
            pltpu.VMEM((c2 // 128, rows, 128), jnp.float32),
            dma(3), dma(3), dma(2), dma(2),
        ],
        part,
    )
    up_pad = up_own[EDGE - 2 : EDGE + rows + 2]
    dec_part = conv_stack(up_pad, w_dec).astype(BF16)
    dec_part = dec_part.reshape(rows, n, c1).transpose(1, 0, 2)
    pred, slope_chan, slope_seq, up_all = call(
        functools.partial(slope_kernel, n, 1.0 / math.sqrt(length)), 2,
        (
            struct((rows, c1), BF16),
            struct((n, rows + 2 * EDGE, c1), BF16),
            struct((n, rows, c1), BF16),
            struct((n, rows, c2), BF16),
        ),
        [
            pltpu.VMEM((n - 1, rows, c1), BF16),
            pltpu.VMEM((rows, c1), BF16),
            pltpu.VMEM((rows, c1), BF16),
            pltpu.VMEM((n, half, c2), BF16),
            pltpu.VMEM((c2 // 128, rows, 128), jnp.float32),
            dma(3), dma(3), dma(3), dma(3), dma(n), dma(n), dma(n), dma(n),
            dma(n), dma(n), dma(n), dma(2),
            *turn_scratch(n),
        ],
        dec_part, stem_pad[2 : 2 + rows], targets, pool,
    )
    slope_pad = jnp.concatenate(
        [slope_chan[j, EDGE - 2 : EDGE + rows + 2] for j in range(n)], axis=1
    )
    up_grad = lax.dot_general(
        windows(slope_pad)[::-1], w_dec, (((0, 2), (1, 0)), ((), ())),
        preferred_element_type=jnp.float32,
    )
    pre_seq = call(
        functools.partial(turn_kernel, n), 3, struct((n, rows, c2), BF16),
        [pltpu.VMEM((rows, c2), BF16), *turn_scratch(n)], up_grad, enc_pre,
    )
    up_all = jnp.pad(up_all.reshape(length, c2), ((2, 2), (0, 0)))
    g_dec = all_rows_grad(slope_seq.reshape(length, c1), up_all)
    g_enc = all_rows_grad(pre_seq.reshape(length, c2), stem_all)
    return (pred, g_enc, g_dec)


def shards(dna_bases, w_stem, w_enc, w_dec, targets):
    args = (dna_bases, w_stem, w_enc, w_dec, targets)
    rows, c1, c2 = dna_bases.shape[0], w_stem.shape[0], w_dec.shape[2]
    n = lax.axis_size("seq")
    square = n == 4 and lax.axis_size("chan") == 4
    if square and rows % 128 == 0 and c2 % 128 == 0 and c1 % 64 == 0:
        return square_shards(*args)
    return general_shards(*args)


def solution(mesh):
    return jax.shard_map(
        shards,
        mesh=mesh,
        in_specs=(
            P(("groups", "seq")),
            P("chan", None, None),
            P(None, None, "chan"),
            P(None, None, "chan"),
            P(("groups", "seq"), "chan"),
        ),
        out_specs=(
            P(("groups", "seq"), "chan"),
            P(("groups", "seq"), None, "chan"),
            P(("groups", "seq"), None, "chan"),
        ),
        check_vma=False,
    )
```

```python
import functools
import math

import jax
import jax.numpy as jnp
from jax import lax
from jax.experimental import pallas as pl
from jax.experimental.pallas import tpu as pltpu
from jax.sharding import PartitionSpec as P

KW = 5


SQRT_TWO_PI = 0.7978845608028654
CUBIC = 0.044715


def extended(block, sides, width):
    for axis, dim in sides:
        count = lax.axis_size(axis)
        forward = [(i, i + 1) for i in range(count - 1)]
        backward = [(target, source) for source, target in forward]
        low = lax.ppermute(
            lax.slice_in_dim(block, block.shape[dim] - width, None, axis=dim), axis, forward
        )
        high = lax.ppermute(lax.slice_in_dim(block, 0, width, axis=dim), axis, backward)
        block = jnp.concatenate([low, block, high], axis=dim)
    return block


def gelu_value(value):
    inner = jnp.tanh(SQRT_TWO_PI * (value + CUBIC * value * value * value))
    return 0.5 * value * (1.0 + inner)


def gelu_slope(value):
    inner = jnp.tanh(SQRT_TWO_PI * (value + CUBIC * value * value * value))
    return 0.5 * (1.0 + inner) + 0.5 * value * (1.0 - inner * inner) * SQRT_TWO_PI * (
        1.0 + 3.0 * CUBIC * value * value
    )


def rim_cells(block, margin):
    return extended(block, (("seq", 0),), margin)


def channel_sum(partial_value):
    return lax.psum_scatter(partial_value, "chan", scatter_dimension=1, tiled=True)


def channel_gather(block):
    return lax.all_gather(block, "chan", axis=1, tiled=True)


def conv_rows(padded, weight):
    row_count = padded.shape[0] - 4
    total = jnp.zeros((row_count, weight.shape[0]), jnp.float32)
    for k in range(KW):
        total = total + lax.dot_general(
            padded[k : k + row_count],
            weight[:, k, :],
            (((1,), (1,)), ((), ())),
            preferred_element_type=jnp.float32,
        )
    return total


def grad_taps(picked, padded):
    row_count = picked.shape[0]
    pieces = [
        lax.dot_general(
            picked,
            padded[k : k + row_count],
            (((0,), (0,)), ((), ())),
            preferred_element_type=jnp.float32,
        )
        for k in range(KW)
    ]
    return jnp.stack(pieces, axis=1)


def weight_grad(cotangent, padded):
    rounded = grad_taps(cotangent, padded).astype(jnp.bfloat16)
    return lax.psum_scatter(
        lax.optimization_barrier(rounded).astype(jnp.float32),
        "seq",
        scatter_dimension=0,
        tiled=True,
    )


def general_shards(dna_bases, w_stem, w_enc, w_dec, targets):
    row_count = dna_bases.shape[0]
    devices = lax.axis_size("seq")
    length = row_count * devices
    onehot = (dna_bases[:, None] == jnp.arange(4, dtype=jnp.int32)[None, :]).astype(jnp.bfloat16)
    onehot_pad = rim_cells(onehot, 2)
    stem_out = gelu_value(conv_rows(onehot_pad, w_stem)).astype(jnp.bfloat16)
    stem_pad = rim_cells(stem_out, 2)
    enc_pre = channel_sum(conv_rows(stem_pad, w_enc))
    active = gelu_value(enc_pre).astype(jnp.bfloat16).astype(jnp.float32)
    pooled = (0.5 * active.reshape(row_count // 2, 2, -1).sum(axis=1)).astype(jnp.bfloat16)
    pooled_pad = rim_cells(pooled, 1)
    up_pad = jnp.repeat(pooled_pad, 2, axis=0)
    output = channel_sum(conv_rows(up_pad, w_dec)) + stem_out.astype(jnp.float32)
    pred = output.astype(jnp.bfloat16)
    scale = 1.0 / math.sqrt(length)
    slope_out = ((output - targets.astype(jnp.float32)) * scale).astype(jnp.bfloat16)
    slope_all = channel_gather(slope_out)
    g_dec = weight_grad(slope_all, up_pad)
    slope_pad = rim_cells(slope_all, 2)
    up_grad = jnp.zeros((row_count, w_dec.shape[2]), jnp.float32)
    for k in range(KW):
        up_grad = up_grad + jnp.dot(
            slope_pad[4 - k : 4 - k + row_count], w_dec[:, k, :], preferred_element_type=jnp.float32
        )
    pool_grad = up_grad.reshape(row_count // 2, 2, -1).sum(axis=1)
    act_grad = 0.5 * jnp.repeat(pool_grad, 2, axis=0)
    pre_grad = (act_grad * gelu_slope(enc_pre)).astype(jnp.bfloat16)
    pre_all = channel_gather(pre_grad)
    g_enc = weight_grad(pre_all, stem_pad)
    return (pred, g_enc, g_dec)


MESH_ID = pl.DeviceIdType.MESH
BF16 = jnp.bfloat16
EDGE = 16
CHUNKS = 4
STEP = 64
VMEM_BYTES = 8 * 1024 * 1024


def send(src, dst, send_sem, recv_sem, seq, chan):
    return pltpu.make_async_remote_copy(
        src_ref=src,
        dst_ref=dst,
        send_sem=send_sem,
        recv_sem=recv_sem,
        device_id={"seq": seq, "chan": chan},
        device_id_type=MESH_ID,
    )


def greet(targets):
    barrier = pltpu.get_barrier_semaphore()
    for seq, chan in targets:
        pl.semaphore_signal(
            barrier, inc=1, device_id={"seq": seq, "chan": chan}, device_id_type=MESH_ID
        )
    pl.semaphore_wait(barrier, len(targets))


def whole_group(n, s, c):
    others = []
    for ds in range(n):
        for dc in range(n):
            if ds or dc:
                others.append((lax.rem(s + ds, n), lax.rem(c + dc, n)))
    return others


def bases_kernel(n, own_ref, all_ref, local_sem, send_sem, recv_sem):
    s, c = lax.axis_index("seq"), lax.axis_index("chan")
    peers = [lax.rem(s + d, n) for d in range(1, n)]
    greet([(p, c) for p in peers])
    copies = [
        send(own_ref, all_ref.at[s], send_sem.at[d], recv_sem.at[d], p, c)
        for d, p in enumerate(peers)
    ]
    for copy in copies:
        copy.start()
    mine = pltpu.make_async_copy(own_ref, all_ref.at[s], local_sem)
    mine.start()
    mine.wait()
    for copy in copies:
        copy.wait()


def partners(c):
    mate = c + 1 - 2 * lax.rem(c, 2)
    across = lax.rem(c + 2, 4)
    return mate, across, lax.rem(mate + 2, 4)


class Turn:
    def __init__(self, n, s, c, own, out, sems):
        self.n, self.s, self.c, self.own, self.out = n, s, c, own, out
        self.quarter_send, self.quarter_recv, self.share_send, self.share_recv, self.local = sems
        self.piece = own.shape[0] // n

    def rows(self, index):
        return pl.ds(pl.multiple_of(index * self.piece, self.piece), self.piece)

    def keep(self):
        at = self.rows(self.c)
        return pltpu.make_async_copy(self.own.at[at], self.out.at[self.s, at], self.local)

    def quarter(self, q, slot):
        at = self.rows(q)
        return send(self.own.at[at], self.out.at[self.s, at], self.quarter_send.at[q],
                    self.quarter_recv.at[slot], self.c, q)

    def each(self, action, mine, before=None):
        for q in range(self.n):
            if before is not None:
                before(q * self.piece)
            itself = jnp.logical_and(self.s == self.c, self.c == q)
            pl.when(jnp.logical_not(itself))(functools.partial(action, q))
        if mine is not None:
            pl.when(self.s == self.c)(mine)

    def start(self, before=None):
        self.each(
            lambda q: self.quarter(q, self.s).start(), lambda: self.keep().start(), before
        )

    def share(self, slot, kind, part, to):
        at = self.rows(part)
        index = slot * 3 + kind
        return send(self.out.at[slot, at], self.out.at[slot, at], self.share_send.at[index],
                    self.share_recv.at[index], self.s, to)

    def slots(self):
        return [lax.rem(self.s + d, self.n) for d in range(self.n)]

    def forward(self):
        mate, across, _ = partners(self.c)
        for d, slot in enumerate(self.slots()):
            if d == 0:
                pl.when(self.s == self.c)(lambda: self.keep().wait())
                pl.when(self.s != self.c)(lambda: self.quarter(self.c, slot).wait_recv())
            else:
                self.quarter(self.c, slot).wait_recv()
            self.share(slot, 1, self.c, across).start()
            self.share(slot, 0, self.c, mate).start()

    def relay(self):
        mate, across, _ = partners(self.c)
        for slot in self.slots():
            self.share(slot, 1, across, across).wait_recv()
            self.share(slot, 2, across, mate).start()

    def finish(self):
        mate, across, far = partners(self.c)
        for slot in self.slots():
            self.share(slot, 0, mate, mate).wait_recv()
            self.share(slot, 2, far, mate).wait_recv()
            self.share(slot, 0, self.c, mate).wait_send()
            self.share(slot, 1, self.c, across).wait_send()
            self.share(slot, 2, across, mate).wait_send()
        self.each(lambda q: self.quarter(q, self.s).wait_send(), None)


def pair_sum(block, held, pair, s, c, rows, send_sem, recv_sem, finish, done):
    mate, across, far = partners(c)
    piece = rows // CHUNKS
    sources = (block(mate), block(far), pair)
    targets = (mate, mate, across)

    def hop(kind, q):
        at = pl.ds(q * piece, piece)
        index = kind * CHUNKS + q
        return send(sources[kind].at[at], held.at[kind, at], send_sem.at[index],
                    recv_sem.at[index], s, targets[kind])

    def steps(q, body):
        @pl.loop(0, piece // STEP)
        def _(i):
            body(pl.ds(pl.multiple_of(q * piece + i * STEP, STEP), STEP))

    def pair_rows(at):
        pair[at, :] = (
            block(across)[at, :].astype(jnp.float32) + held[1, at, :].astype(jnp.float32)
        ).astype(BF16)

    def total_rows(at):
        total = block(c)[at, :].astype(jnp.float32) + held[0, at, :].astype(jnp.float32)
        finish(at, total + held[2, at, :].astype(jnp.float32))

    for q in range(CHUNKS):
        hop(1, q).start()
    for q in range(CHUNKS):
        hop(0, q).start()
    for q in range(CHUNKS):
        hop(1, q).wait_recv()
        steps(q, pair_rows)
        hop(2, q).start()
    for q in range(CHUNKS):
        hop(0, q).wait_recv()
        hop(2, q).wait_recv()
        steps(q, total_rows)
        done(q)
    return [hop(kind, q) for kind in range(3) for q in range(CHUNKS)]


def pair_add(value):
    count = value.shape[0]
    row = lax.broadcasted_iota(jnp.int32, value.shape, 0)
    other = jnp.where(
        lax.rem(row, 2) == 0, pltpu.roll(value, count - 1, 0), pltpu.roll(value, 1, 0)
    )
    return value + other


def encoder_kernel(
    n, part_ref, pre_ref, up_ref, pool_ref, held, pair, wide,
    send_sem, recv_sem, edge_send, edge_recv,
):
    s, c = lax.axis_index("seq"), lax.axis_index("chan")
    rows, width = pre_ref.shape
    half = rows // 2
    greet(
        [(s, lax.rem(c + d, n)) for d in range(1, n)]
        + [(lax.rem(s + d, n), c) for d in range(1, n)]
    )

    def block(j):
        return part_ref.at[:, pl.ds(pl.multiple_of(j * width, 128), width)]

    def finish(at, total):
        pre_ref[at, :] = total
        active = gelu_value(total).astype(BF16).astype(jnp.float32)
        pooled = (0.5 * pair_add(active)).astype(BF16)
        up_ref[pl.ds(pl.multiple_of(at.start + EDGE, EDGE), at.size), :] = pooled
        for j in range(width // 128):
            wide[j, at, :] = pooled[:, j * 128 : (j + 1) * 128].astype(jnp.float32)

    copies = pair_sum(
        block, held, pair, s, c, rows, send_sem, recv_sem, finish, lambda q: None
    )
    up = send(up_ref.at[pl.ds(rows, EDGE)], up_ref.at[pl.ds(0, EDGE)], edge_send.at[0],
              edge_recv.at[0], lax.rem(s + 1, n), c)
    down = send(up_ref.at[pl.ds(EDGE, EDGE)], up_ref.at[pl.ds(rows + EDGE, EDGE)],
                edge_send.at[1], edge_recv.at[1], lax.rem(s + n - 1, n), c)
    up.start()
    down.start()
    for j in range(width // 128):
        pool_ref[:, j * 128 : (j + 1) * 128] = wide[j, pl.ds(0, half, stride=2), :].astype(BF16)
    up.wait()
    down.wait()
    blank = jnp.zeros((EDGE, width), BF16)

    @pl.when(s == 0)
    def _():
        up_ref[0:EDGE, :] = blank

    @pl.when(s == n - 1)
    def _():
        up_ref[rows + EDGE :, :] = blank

    for copy in copies:
        copy.wait_send()


class PoolRelay:
    def __init__(self, n, s, c, own, out, right_send, left_send, recv, local):
        self.n, self.s, self.c, self.own, self.out = n, s, c, own, out
        self.right_send, self.left_send, self.recv = right_send, left_send, recv
        self.mine = pltpu.make_async_copy(own, out.at[s], local)

    def hop(self, src, slot, step):
        sems = self.right_send if step > 0 else self.left_send
        return send(src, self.out.at[slot], sems.at[slot], self.recv.at[slot], self.s + step, self.c)

    def start(self):
        pl.when(self.s < self.n - 1)(lambda: self.hop(self.own, self.s, 1).start())
        pl.when(self.s > 0)(lambda: self.hop(self.own, self.s, -1).start())
        self.mine.start()

    def arrive(self, d):
        low, high = self.s - d, self.s + d

        @pl.when(low >= 0)
        def _():
            self.hop(self.out.at[low], low, 1).wait_recv()
            pl.when(self.s < self.n - 1)(lambda: self.hop(self.out.at[low], low, 1).start())

        @pl.when(high < self.n)
        def _():
            self.hop(self.out.at[high], high, -1).wait_recv()
            pl.when(self.s > 0)(lambda: self.hop(self.out.at[high], high, -1).start())

    def end(self):
        self.mine.wait()
        for slot in range(self.n):
            pl.when(jnp.logical_and(slot <= self.s, self.s < self.n - 1))(
                lambda: self.hop(self.own, slot, 1).wait_send()
            )
            pl.when(jnp.logical_and(slot >= self.s, self.s > 0))(
                lambda: self.hop(self.own, slot, -1).wait_send()
            )


def slope_kernel(
    n, scale, part_ref, stem_ref, target_ref, pool_ref, pred_ref, chan_ref, all_ref,
    held, pair, send_sem, recv_sem, row_send, row_recv, lo_send, lo_recv, hi_send, hi_recv,
    right_send, left_send, pool_recv, local_sem,
):
    s, c = lax.axis_index("seq"), lax.axis_index("chan")
    rows, width = pred_ref.shape
    piece = rows // CHUNKS
    mate, across, far = partners(c)
    greet(whole_group(n, s, c))
    pools = PoolRelay(n, s, c, pool_ref, all_ref, right_send, left_send, pool_recv, local_sem)
    up, down = lax.rem(s + 1, n), lax.rem(s + n - 1, n)

    def finish(at, total):
        output = total + stem_ref[at, :].astype(jnp.float32)
        pred_ref[at, :] = output.astype(BF16)
        spot = pl.ds(pl.multiple_of(at.start + EDGE, EDGE), at.size)
        chan_ref[c, spot, :] = ((output - target_ref[at, :].astype(jnp.float32)) * scale).astype(BF16)

    def row_copy(kind, q, owner, to):
        spot = chan_ref.at[owner, pl.ds(EDGE + q * piece, piece)]
        index = kind * CHUNKS + q
        return send(spot, spot, row_send.at[index], row_recv.at[index], s, to)

    lo_copies, hi_copies = [], []
    for d in range(n):
        p = lax.rem(c + d, n)
        lo_copies.append(
            send(chan_ref.at[c, pl.ds(rows, EDGE)], chan_ref.at[c, pl.ds(0, EDGE)],
                 lo_send.at[d], lo_recv.at[d], up, p)
        )
        hi_copies.append(
            send(chan_ref.at[c, pl.ds(EDGE, EDGE)], chan_ref.at[c, pl.ds(EDGE + rows, EDGE)],
                 hi_send.at[d], hi_recv.at[d], down, p)
        )

    def done(q):
        row_copy(1, q, c, across).start()
        row_copy(0, q, c, mate).start()
        if q == 0:
            for copy in hi_copies:
                copy.start()
        if q == CHUNKS - 1:
            for copy in lo_copies:
                copy.start()

    pools.start()
    copies = pair_sum(
        lambda j: part_ref.at[j], held, pair, s, c, rows, send_sem, recv_sem, finish, done
    )
    pools.arrive(1)
    for q in range(CHUNKS):
        row_copy(1, q, across, across).wait_recv()
        row_copy(2, q, across, mate).start()
    pools.arrive(2)
    for q in range(CHUNKS):
        row_copy(0, q, mate, mate).wait_recv()
        row_copy(2, q, far, mate).wait_recv()
    for copy in lo_copies + hi_copies:
        copy.wait()
    blank = jnp.zeros((EDGE, width), BF16)

    @pl.when(s == 0)
    def _():
        for j in range(n):
            chan_ref[j, 0:EDGE, :] = blank

    @pl.when(s == n - 1)
    def _():
        for j in range(n):
            chan_ref[j, EDGE + rows :, :] = blank

    pools.arrive(3)
    pools.end()
    for q in range(CHUNKS):
        row_copy(0, q, c, mate).wait_send()
        row_copy(1, q, c, across).wait_send()
        row_copy(2, q, across, mate).wait_send()
    for copy in copies:
        copy.wait_send()


def turn_kernel(
    n, grad_ref, pre_ref, chan_ref, all_ref, pre_seq_ref, slope_seq_ref, up_ref, own, wide, *sems
):
    s, c = lax.axis_index("seq"), lax.axis_index("chan")
    rows = own.shape[0]
    half, up_width = all_ref.shape[1:]
    greet(whole_group(n, s, c))
    slope_own = chan_ref.at[c, pl.ds(EDGE, rows)]
    slope_turn = Turn(n, s, c, slope_own, slope_seq_ref, sems[: len(sems) // 2])
    turn = Turn(n, s, c, own, pre_seq_ref, sems[len(sems) // 2 :])

    def pre_rows(first):
        @pl.loop(0, turn.piece // STEP)
        def _(i):
            at = pl.ds(pl.multiple_of(first + i * STEP, STEP), STEP)
            grad = 0.5 * pair_add(grad_ref[at, :])
            own[at, :] = (grad * gelu_slope(pre_ref[at, :])).astype(BF16)

    slope_turn.start()
    turn.start(pre_rows)
    slope_turn.forward()
    turn.forward()

    @pl.loop(0, n)
    def _(slot):
        for j in range(up_width // 128):
            lanes = slice(j * 128, (j + 1) * 128)
            value = all_ref[slot, :, lanes].astype(jnp.float32)
            wide[j, pl.ds(0, half, stride=2), :] = value
            wide[j, pl.ds(1, half, stride=2), :] = value
            up_ref[slot, :, lanes] = wide[j].astype(BF16)

    slope_turn.relay()
    turn.relay()
    slope_turn.finish()
    turn.finish()


def turn_scratch(n):
    return [dma(n), dma(n), dma(3 * n), dma(3 * n), pltpu.SemaphoreType.DMA]


def call(kernel, ident, outs, scratch, *operands):
    vmem = pl.BlockSpec(memory_space=pltpu.VMEM)
    return pl.pallas_call(
        kernel,
        out_shape=outs,
        in_specs=[vmem] * len(operands),
        out_specs=jax.tree.map(lambda _: vmem, outs),
        scratch_shapes=scratch,
        compiler_params=pltpu.CompilerParams(
            collective_id=ident, has_side_effects=True, vmem_limit_bytes=VMEM_BYTES
        ),
    )(*operands)


def dma(count):
    return pltpu.SemaphoreType.DMA((count,))


def windows(padded):
    count = padded.shape[0] - 4
    return jnp.stack([padded[k : k + count] for k in range(KW)], axis=0)


def conv_stack(padded, weight):
    return lax.dot_general(
        windows(padded), weight, (((0, 2), (1, 2)), ((), ())), preferred_element_type=jnp.float32
    )


def all_rows_grad(cotangent, padded):
    count = cotangent.shape[0]
    pieces = [
        lax.dot_general(
            cotangent, padded[k : k + count], (((0,), (0,)), ((), ())),
            preferred_element_type=jnp.float32,
        )
        for k in range(KW)
    ]
    return jnp.stack(pieces, axis=1)


def square_shards(dna_bases, w_stem, w_enc, w_dec, targets):
    rows = dna_bases.shape[0]
    n = lax.axis_size("seq")
    length = rows * n
    s = lax.axis_index("seq")
    c1, c2 = w_stem.shape[0], w_dec.shape[2]
    struct = jax.ShapeDtypeStruct
    bases = call(
        functools.partial(bases_kernel, n), 0, struct((n, rows // 128, 128), jnp.int32),
        [pltpu.SemaphoreType.DMA, dma(n - 1), dma(n - 1)], dna_bases.reshape(rows // 128, 128),
    ).reshape(length)
    bases_pad = jnp.pad(bases, (2, 2), constant_values=-1)
    shifts = jnp.stack([bases_pad[k : k + length] for k in range(KW)])
    onehot = (shifts[:, None, :] == jnp.arange(4, dtype=jnp.int32)[None, :, None]).astype(BF16)
    stem_pre = lax.dot_general(
        onehot.reshape(KW * 4, length), w_stem.reshape(c1, KW * 4), (((0,), (1,)), ((), ())),
        preferred_element_type=jnp.float32,
    )
    stem_all = jnp.pad(gelu_value(stem_pre).astype(BF16), ((2, 2), (0, 0)))
    stem_pad = lax.dynamic_slice_in_dim(stem_all, s * rows, rows + 4, 0)
    part = conv_stack(stem_pad, w_enc).astype(BF16)
    half = rows // 2
    enc_pre, up_own, pool = call(
        functools.partial(encoder_kernel, n), 1,
        (
            struct((rows, c2), jnp.float32),
            struct((rows + 2 * EDGE, c2), BF16),
            struct((half, c2), BF16),
        ),
        [
            pltpu.VMEM((n - 1, rows, c2), BF16),
            pltpu.VMEM((rows, c2), BF16),
            pltpu.VMEM((c2 // 128, rows, 128), jnp.float32),
            dma(3 * CHUNKS), dma(3 * CHUNKS), dma(2), dma(2),
        ],
        part,
    )
    up_pad = up_own[EDGE - 2 : EDGE + rows + 2]
    dec_part = jnp.stack(
        [conv_stack(up_pad, w_dec[j * c1 : (j + 1) * c1]).astype(BF16) for j in range(n)]
    )
    pred, slope_chan, pool_all = call(
        functools.partial(slope_kernel, n, 1.0 / math.sqrt(length)), 2,
        (
            struct((rows, c1), BF16),
            struct((n, rows + 2 * EDGE, c1), BF16),
            struct((n, half, c2), BF16),
        ),
        [
            pltpu.VMEM((n - 1, rows, c1), BF16),
            pltpu.VMEM((rows, c1), BF16),
            dma(3 * CHUNKS), dma(3 * CHUNKS), dma(3 * CHUNKS), dma(3 * CHUNKS),
            dma(n), dma(n), dma(n), dma(n), dma(n), dma(n), dma(n),
            pltpu.SemaphoreType.DMA,
        ],
        dec_part, stem_pad[2 : 2 + rows], targets, pool,
    )
    slope_pad = jnp.concatenate(
        [slope_chan[j, EDGE - 2 : EDGE + rows + 2] for j in range(n)], axis=1
    )
    up_grad = jnp.zeros((rows, c2), jnp.float32)
    for k in range(KW):
        up_grad = up_grad + jnp.dot(
            slope_pad[4 - k : 4 - k + rows], w_dec[:, k, :], preferred_element_type=jnp.float32
        )
    pre_seq, slope_seq, up_all = call(
        functools.partial(turn_kernel, n), 3,
        (
            struct((n, rows, c2), BF16),
            struct((n, rows, c1), BF16),
            struct((n, rows, c2), BF16),
        ),
        [
            pltpu.VMEM((rows, c2), BF16),
            pltpu.VMEM((c2 // 128, rows, 128), jnp.float32),
            *turn_scratch(n), *turn_scratch(n),
        ],
        up_grad, enc_pre, slope_chan, pool_all,
    )
    up_all = jnp.pad(up_all.reshape(length, c2), ((2, 2), (0, 0)))
    g_dec = all_rows_grad(slope_seq.reshape(length, c1), up_all)
    g_enc = all_rows_grad(pre_seq.reshape(length, c2), stem_all)
    return (pred, g_enc, g_dec)


def shards(dna_bases, w_stem, w_enc, w_dec, targets):
    args = (dna_bases, w_stem, w_enc, w_dec, targets)
    rows, c1, c2 = dna_bases.shape[0], w_stem.shape[0], w_dec.shape[2]
    n = lax.axis_size("seq")
    square = n == 4 and lax.axis_size("chan") == 4
    if square and rows % (CHUNKS * STEP) == 0 and c2 % 128 == 0 and c1 % 64 == 0:
        return square_shards(*args)
    return general_shards(*args)


def solution(mesh):
    return jax.shard_map(
        shards,
        mesh=mesh,
        in_specs=(
            P(("groups", "seq")),
            P("chan", None, None),
            P(None, None, "chan"),
            P(None, None, "chan"),
            P(("groups", "seq"), "chan"),
        ),
        out_specs=(
            P(("groups", "seq"), "chan"),
            P(("groups", "seq"), None, "chan"),
            P(("groups", "seq"), None, "chan"),
        ),
        check_vma=False,
    )
```

```python
import functools
import math

import jax
import jax.numpy as jnp
from jax import lax
from jax.experimental import pallas as pl
from jax.experimental.pallas import tpu as pltpu
from jax.sharding import PartitionSpec as P

KW = 5


SQRT_TWO_PI = 0.7978845608028654
CUBIC = 0.044715


def extended(block, sides, width):
    for axis, dim in sides:
        count = lax.axis_size(axis)
        forward = [(i, i + 1) for i in range(count - 1)]
        backward = [(target, source) for source, target in forward]
        low = lax.ppermute(
            lax.slice_in_dim(block, block.shape[dim] - width, None, axis=dim), axis, forward
        )
        high = lax.ppermute(lax.slice_in_dim(block, 0, width, axis=dim), axis, backward)
        block = jnp.concatenate([low, block, high], axis=dim)
    return block


def gelu_value(value):
    inner = jnp.tanh(SQRT_TWO_PI * (value + CUBIC * value * value * value))
    return 0.5 * value * (1.0 + inner)


def gelu_slope(value):
    inner = jnp.tanh(SQRT_TWO_PI * (value + CUBIC * value * value * value))
    return 0.5 * (1.0 + inner) + 0.5 * value * (1.0 - inner * inner) * SQRT_TWO_PI * (
        1.0 + 3.0 * CUBIC * value * value
    )


def rim_cells(block, margin):
    return extended(block, (("seq", 0),), margin)


def channel_sum(partial_value):
    return lax.psum_scatter(partial_value, "chan", scatter_dimension=1, tiled=True)


def channel_gather(block):
    return lax.all_gather(block, "chan", axis=1, tiled=True)


def conv_rows(padded, weight):
    row_count = padded.shape[0] - 4
    total = jnp.zeros((row_count, weight.shape[0]), jnp.float32)
    for k in range(KW):
        total = total + lax.dot_general(
            padded[k : k + row_count],
            weight[:, k, :],
            (((1,), (1,)), ((), ())),
            preferred_element_type=jnp.float32,
        )
    return total


def grad_taps(picked, padded):
    row_count = picked.shape[0]
    pieces = [
        lax.dot_general(
            picked,
            padded[k : k + row_count],
            (((0,), (0,)), ((), ())),
            preferred_element_type=jnp.float32,
        )
        for k in range(KW)
    ]
    return jnp.stack(pieces, axis=1)


def weight_grad(cotangent, padded):
    rounded = grad_taps(cotangent, padded).astype(jnp.bfloat16)
    return lax.psum_scatter(
        lax.optimization_barrier(rounded).astype(jnp.float32),
        "seq",
        scatter_dimension=0,
        tiled=True,
    )


def general_shards(dna_bases, w_stem, w_enc, w_dec, targets):
    row_count = dna_bases.shape[0]
    devices = lax.axis_size("seq")
    length = row_count * devices
    onehot = (dna_bases[:, None] == jnp.arange(4, dtype=jnp.int32)[None, :]).astype(jnp.bfloat16)
    onehot_pad = rim_cells(onehot, 2)
    stem_out = gelu_value(conv_rows(onehot_pad, w_stem)).astype(jnp.bfloat16)
    stem_pad = rim_cells(stem_out, 2)
    enc_pre = channel_sum(conv_rows(stem_pad, w_enc))
    active = gelu_value(enc_pre).astype(jnp.bfloat16).astype(jnp.float32)
    pooled = (0.5 * active.reshape(row_count // 2, 2, -1).sum(axis=1)).astype(jnp.bfloat16)
    pooled_pad = rim_cells(pooled, 1)
    up_pad = jnp.repeat(pooled_pad, 2, axis=0)
    output = channel_sum(conv_rows(up_pad, w_dec)) + stem_out.astype(jnp.float32)
    pred = output.astype(jnp.bfloat16)
    scale = 1.0 / math.sqrt(length)
    slope_out = ((output - targets.astype(jnp.float32)) * scale).astype(jnp.bfloat16)
    slope_all = channel_gather(slope_out)
    g_dec = weight_grad(slope_all, up_pad)
    slope_pad = rim_cells(slope_all, 2)
    up_grad = jnp.zeros((row_count, w_dec.shape[2]), jnp.float32)
    for k in range(KW):
        up_grad = up_grad + jnp.dot(
            slope_pad[4 - k : 4 - k + row_count], w_dec[:, k, :], preferred_element_type=jnp.float32
        )
    pool_grad = up_grad.reshape(row_count // 2, 2, -1).sum(axis=1)
    act_grad = 0.5 * jnp.repeat(pool_grad, 2, axis=0)
    pre_grad = (act_grad * gelu_slope(enc_pre)).astype(jnp.bfloat16)
    pre_all = channel_gather(pre_grad)
    g_enc = weight_grad(pre_all, stem_pad)
    return (pred, g_enc, g_dec)


MESH_ID = pl.DeviceIdType.MESH
BF16 = jnp.bfloat16
EDGE = 16
CHUNKS = 4
STEP = 64
VMEM_BYTES = 8 * 1024 * 1024


def send(src, dst, send_sem, recv_sem, seq, chan):
    return pltpu.make_async_remote_copy(
        src_ref=src,
        dst_ref=dst,
        send_sem=send_sem,
        recv_sem=recv_sem,
        device_id={"seq": seq, "chan": chan},
        device_id_type=MESH_ID,
    )


def greet(targets):
    barrier = pltpu.get_barrier_semaphore()
    for seq, chan in targets:
        pl.semaphore_signal(
            barrier, inc=1, device_id={"seq": seq, "chan": chan}, device_id_type=MESH_ID
        )
    pl.semaphore_wait(barrier, len(targets))


def whole_group(n, s, c):
    others = []
    for ds in range(n):
        for dc in range(n):
            if ds or dc:
                others.append((lax.rem(s + ds, n), lax.rem(c + dc, n)))
    return others


def bases_kernel(n, own_ref, all_ref, local_sem, send_sem, recv_sem):
    s, c = lax.axis_index("seq"), lax.axis_index("chan")
    peers = [lax.rem(s + d, n) for d in range(1, n)]
    greet([(p, c) for p in peers])
    copies = [
        send(own_ref, all_ref.at[s], send_sem.at[d], recv_sem.at[d], p, c)
        for d, p in enumerate(peers)
    ]
    for copy in copies:
        copy.start()
    mine = pltpu.make_async_copy(own_ref, all_ref.at[s], local_sem)
    mine.start()
    mine.wait()
    for copy in copies:
        copy.wait()


def partners(c):
    mate = c + 1 - 2 * lax.rem(c, 2)
    across = lax.rem(c + 2, 4)
    return mate, across, lax.rem(mate + 2, 4)


class Turn:
    def __init__(self, n, s, c, own, out, sems):
        self.n, self.s, self.c, self.own, self.out = n, s, c, own, out
        self.quarter_send, self.quarter_recv, self.share_send, self.share_recv, self.local = sems
        self.piece = own.shape[0] // n

    def rows(self, index):
        return pl.ds(pl.multiple_of(index * self.piece, self.piece), self.piece)

    def keep(self):
        at = self.rows(self.c)
        return pltpu.make_async_copy(self.own.at[at], self.out.at[self.s, at], self.local)

    def quarter(self, q, slot):
        at = self.rows(q)
        return send(self.own.at[at], self.out.at[self.s, at], self.quarter_send.at[q],
                    self.quarter_recv.at[slot], self.c, q)

    def each(self, action, mine, before=None):
        for q in range(self.n):
            if before is not None:
                before(q * self.piece)
            itself = jnp.logical_and(self.s == self.c, self.c == q)
            pl.when(jnp.logical_not(itself))(functools.partial(action, q))
        if mine is not None:
            pl.when(self.s == self.c)(mine)

    def start(self, before=None):
        self.each(
            lambda q: self.quarter(q, self.s).start(), lambda: self.keep().start(), before
        )

    def share(self, slot, kind, part, to):
        at = self.rows(part)
        index = slot * 3 + kind
        return send(self.out.at[slot, at], self.out.at[slot, at], self.share_send.at[index],
                    self.share_recv.at[index], self.s, to)

    def slots(self):
        return [lax.rem(self.s + d, self.n) for d in range(self.n)]

    def forward(self):
        mate, across, _ = partners(self.c)
        for d, slot in enumerate(self.slots()):
            if d == 0:
                pl.when(self.s == self.c)(lambda: self.keep().wait())
                pl.when(self.s != self.c)(lambda: self.quarter(self.c, slot).wait_recv())
            else:
                self.quarter(self.c, slot).wait_recv()
            self.share(slot, 1, self.c, across).start()
            self.share(slot, 0, self.c, mate).start()

    def relay(self):
        mate, across, _ = partners(self.c)
        for slot in self.slots():
            self.share(slot, 1, across, across).wait_recv()
            self.share(slot, 2, across, mate).start()

    def finish(self):
        mate, across, far = partners(self.c)
        for slot in self.slots():
            self.share(slot, 0, mate, mate).wait_recv()
            self.share(slot, 2, far, mate).wait_recv()
            self.share(slot, 0, self.c, mate).wait_send()
            self.share(slot, 1, self.c, across).wait_send()
            self.share(slot, 2, across, mate).wait_send()
        self.each(lambda q: self.quarter(q, self.s).wait_send(), None)


def pair_sum(block, held, pair, s, c, rows, send_sem, recv_sem, finish, done):
    mate, across, far = partners(c)
    piece = rows // CHUNKS
    sources = (block(mate), block(far), pair)
    targets = (mate, mate, across)

    def hop(kind, q):
        at = pl.ds(q * piece, piece)
        index = kind * CHUNKS + q
        return send(sources[kind].at[at], held.at[kind, at], send_sem.at[index],
                    recv_sem.at[index], s, targets[kind])

    def steps(q, body):
        @pl.loop(0, piece // STEP)
        def _(i):
            body(pl.ds(pl.multiple_of(q * piece + i * STEP, STEP), STEP))

    def pair_rows(at):
        pair[at, :] = (
            block(across)[at, :].astype(jnp.float32) + held[1, at, :].astype(jnp.float32)
        ).astype(BF16)

    def total_rows(at):
        total = block(c)[at, :].astype(jnp.float32) + held[0, at, :].astype(jnp.float32)
        finish(at, total + held[2, at, :].astype(jnp.float32))

    for q in range(CHUNKS):
        hop(1, q).start()
    for q in range(CHUNKS):
        hop(0, q).start()
    for q in range(CHUNKS):
        hop(1, q).wait_recv()
        steps(q, pair_rows)
        hop(2, q).start()
    for q in range(CHUNKS):
        hop(0, q).wait_recv()
        hop(2, q).wait_recv()
        steps(q, total_rows)
        done(q)
    return [hop(kind, q) for kind in range(3) for q in range(CHUNKS)]


def pair_add(value):
    count = value.shape[0]
    row = lax.broadcasted_iota(jnp.int32, value.shape, 0)
    other = jnp.where(
        lax.rem(row, 2) == 0, pltpu.roll(value, count - 1, 0), pltpu.roll(value, 1, 0)
    )
    return value + other


def encoder_kernel(
    n, part_ref, pre_ref, up_ref, pool_ref, held, pair, wide,
    send_sem, recv_sem, edge_send, edge_recv,
):
    s, c = lax.axis_index("seq"), lax.axis_index("chan")
    rows, width = pre_ref.shape
    half = rows // 2
    greet(
        [(s, lax.rem(c + d, n)) for d in range(1, n)]
        + [(lax.rem(s + d, n), c) for d in range(1, n)]
    )

    def block(j):
        return part_ref.at[:, pl.ds(pl.multiple_of(j * width, 128), width)]

    def finish(at, total):
        pre_ref[at, :] = total
        active = gelu_value(total).astype(BF16).astype(jnp.float32)
        pooled = (0.5 * pair_add(active)).astype(BF16)
        up_ref[pl.ds(pl.multiple_of(at.start + EDGE, EDGE), at.size), :] = pooled
        for j in range(width // 128):
            wide[j, at, :] = pooled[:, j * 128 : (j + 1) * 128].astype(jnp.float32)

    copies = pair_sum(
        block, held, pair, s, c, rows, send_sem, recv_sem, finish, lambda q: None
    )
    up = send(up_ref.at[pl.ds(rows, EDGE)], up_ref.at[pl.ds(0, EDGE)], edge_send.at[0],
              edge_recv.at[0], lax.rem(s + 1, n), c)
    down = send(up_ref.at[pl.ds(EDGE, EDGE)], up_ref.at[pl.ds(rows + EDGE, EDGE)],
                edge_send.at[1], edge_recv.at[1], lax.rem(s + n - 1, n), c)
    up.start()
    down.start()
    for j in range(width // 128):
        pool_ref[:, j * 128 : (j + 1) * 128] = wide[j, pl.ds(0, half, stride=2), :].astype(BF16)
    up.wait()
    down.wait()
    blank = jnp.zeros((EDGE, width), BF16)

    @pl.when(s == 0)
    def _():
        up_ref[0:EDGE, :] = blank

    @pl.when(s == n - 1)
    def _():
        up_ref[rows + EDGE :, :] = blank

    for copy in copies:
        copy.wait_send()


class PoolRelay:
    def __init__(self, n, s, c, own, out, right_send, left_send, recv, local):
        self.n, self.s, self.c, self.own, self.out = n, s, c, own, out
        self.right_send, self.left_send, self.recv = right_send, left_send, recv
        self.mine = pltpu.make_async_copy(own, out.at[s], local)

    def hop(self, src, slot, step):
        sems = self.right_send if step > 0 else self.left_send
        return send(src, self.out.at[slot], sems.at[slot], self.recv.at[slot], self.s + step, self.c)

    def start(self):
        pl.when(self.s < self.n - 1)(lambda: self.hop(self.own, self.s, 1).start())
        pl.when(self.s > 0)(lambda: self.hop(self.own, self.s, -1).start())
        self.mine.start()

    def arrive(self, d):
        low, high = self.s - d, self.s + d

        @pl.when(low >= 0)
        def _():
            self.hop(self.out.at[low], low, 1).wait_recv()
            pl.when(self.s < self.n - 1)(lambda: self.hop(self.out.at[low], low, 1).start())

        @pl.when(high < self.n)
        def _():
            self.hop(self.out.at[high], high, -1).wait_recv()
            pl.when(self.s > 0)(lambda: self.hop(self.out.at[high], high, -1).start())

    def end(self):
        self.mine.wait()
        for slot in range(self.n):
            pl.when(jnp.logical_and(slot <= self.s, self.s < self.n - 1))(
                lambda: self.hop(self.own, slot, 1).wait_send()
            )
            pl.when(jnp.logical_and(slot >= self.s, self.s > 0))(
                lambda: self.hop(self.own, slot, -1).wait_send()
            )


def slope_kernel(
    n, scale, part_ref, stem_ref, target_ref, pool_ref, pred_ref, chan_ref, all_ref,
    held, pair, send_sem, recv_sem, row_send, row_recv, lo_send, lo_recv, hi_send, hi_recv,
    right_send, left_send, pool_recv, local_sem,
):
    s, c = lax.axis_index("seq"), lax.axis_index("chan")
    rows, width = pred_ref.shape
    piece = rows // CHUNKS
    mate, across, far = partners(c)
    greet(whole_group(n, s, c))
    pools = PoolRelay(n, s, c, pool_ref, all_ref, right_send, left_send, pool_recv, local_sem)
    up, down = lax.rem(s + 1, n), lax.rem(s + n - 1, n)

    def finish(at, total):
        output = total + stem_ref[at, :].astype(jnp.float32)
        pred_ref[at, :] = output.astype(BF16)
        spot = pl.ds(pl.multiple_of(at.start + EDGE, EDGE), at.size)
        chan_ref[c, spot, :] = ((output - target_ref[at, :].astype(jnp.float32)) * scale).astype(BF16)

    def row_copy(kind, q, owner, to):
        spot = chan_ref.at[owner, pl.ds(EDGE + q * piece, piece)]
        index = kind * CHUNKS + q
        return send(spot, spot, row_send.at[index], row_recv.at[index], s, to)

    lo_copies, hi_copies = [], []
    for d in range(n):
        p = lax.rem(c + d, n)
        lo_copies.append(
            send(chan_ref.at[c, pl.ds(rows, EDGE)], chan_ref.at[c, pl.ds(0, EDGE)],
                 lo_send.at[d], lo_recv.at[d], up, p)
        )
        hi_copies.append(
            send(chan_ref.at[c, pl.ds(EDGE, EDGE)], chan_ref.at[c, pl.ds(EDGE + rows, EDGE)],
                 hi_send.at[d], hi_recv.at[d], down, p)
        )

    def done(q):
        row_copy(1, q, c, across).start()
        row_copy(0, q, c, mate).start()
        if q == 0:
            for copy in hi_copies:
                copy.start()
        if q == CHUNKS - 1:
            for copy in lo_copies:
                copy.start()

    pools.start()
    copies = pair_sum(
        lambda j: part_ref.at[j], held, pair, s, c, rows, send_sem, recv_sem, finish, done
    )
    pools.arrive(1)
    for q in range(CHUNKS):
        row_copy(1, q, across, across).wait_recv()
        row_copy(2, q, across, mate).start()
    pools.arrive(2)
    for q in range(CHUNKS):
        row_copy(0, q, mate, mate).wait_recv()
        row_copy(2, q, far, mate).wait_recv()
    for copy in lo_copies + hi_copies:
        copy.wait()
    blank = jnp.zeros((EDGE, width), BF16)

    @pl.when(s == 0)
    def _():
        for j in range(n):
            chan_ref[j, 0:EDGE, :] = blank

    @pl.when(s == n - 1)
    def _():
        for j in range(n):
            chan_ref[j, EDGE + rows :, :] = blank

    pools.arrive(3)
    pools.end()
    for q in range(CHUNKS):
        row_copy(0, q, c, mate).wait_send()
        row_copy(1, q, c, across).wait_send()
        row_copy(2, q, across, mate).wait_send()
    for copy in copies:
        copy.wait_send()


def turn_kernel(
    n, w_ref, pre_ref, chan_ref, all_ref, pre_seq_ref, slope_seq_ref, up_ref, own, wide, total,
    *sems,
):
    s, c = lax.axis_index("seq"), lax.axis_index("chan")
    rows = own.shape[0]
    half, up_width = all_ref.shape[1:]
    greet(whole_group(n, s, c))
    slope_own = chan_ref.at[c, pl.ds(EDGE, rows)]
    slope_turn = Turn(n, s, c, slope_own, slope_seq_ref, sems[: len(sems) // 2])
    turn = Turn(n, s, c, own, pre_seq_ref, sems[len(sems) // 2 :])

    width = chan_ref.shape[2]
    piece = turn.piece

    def pre_rows(first):
        if first == 2 * piece:
            slope_turn.forward()
        if first == 3 * piece:
            slope_turn.relay()
        total[...] = jnp.zeros_like(total)

        @pl.loop(0, n)
        def _(j):
            window = chan_ref[j, first : first + piece + 2 * EDGE, :].astype(jnp.float32)
            inputs = pl.ds(pl.multiple_of(j * width, EDGE), width)
            part = total[...]
            for k in range(KW):
                start = EDGE + 2 - k
                part = part + jnp.dot(
                    window[start : start + piece].astype(BF16), w_ref[k, inputs, :],
                    preferred_element_type=jnp.float32,
                )
            total[...] = part

        @pl.loop(0, piece // STEP)
        def _(i):
            local = pl.ds(pl.multiple_of(i * STEP, STEP), STEP)
            at = pl.ds(pl.multiple_of(first + i * STEP, STEP), STEP)
            grad = 0.5 * pair_add(total[local, :])
            own[at, :] = (grad * gelu_slope(pre_ref[at, :])).astype(BF16)

    slope_turn.start()
    turn.start(pre_rows)
    turn.forward()

    @pl.loop(0, n)
    def _(slot):
        for j in range(up_width // 128):
            lanes = slice(j * 128, (j + 1) * 128)
            value = all_ref[slot, :, lanes].astype(jnp.float32)
            wide[j, pl.ds(0, half, stride=2), :] = value
            wide[j, pl.ds(1, half, stride=2), :] = value
            up_ref[slot, :, lanes] = wide[j].astype(BF16)

    turn.relay()
    slope_turn.finish()
    turn.finish()


def turn_scratch(n):
    return [dma(n), dma(n), dma(3 * n), dma(3 * n), pltpu.SemaphoreType.DMA]


def call(kernel, ident, outs, scratch, *operands):
    vmem = pl.BlockSpec(memory_space=pltpu.VMEM)
    return pl.pallas_call(
        kernel,
        out_shape=outs,
        in_specs=[vmem] * len(operands),
        out_specs=jax.tree.map(lambda _: vmem, outs),
        scratch_shapes=scratch,
        compiler_params=pltpu.CompilerParams(
            collective_id=ident, has_side_effects=True, vmem_limit_bytes=VMEM_BYTES
        ),
    )(*operands)


def dma(count):
    return pltpu.SemaphoreType.DMA((count,))


def windows(padded):
    count = padded.shape[0] - 4
    return jnp.stack([padded[k : k + count] for k in range(KW)], axis=0)


def conv_stack(padded, weight):
    return lax.dot_general(
        windows(padded), weight, (((0, 2), (1, 2)), ((), ())), preferred_element_type=jnp.float32
    )


def all_rows_grad(cotangent, padded):
    count = cotangent.shape[0]
    pieces = [
        lax.dot_general(
            cotangent, padded[k : k + count], (((0,), (0,)), ((), ())),
            preferred_element_type=jnp.float32,
        )
        for k in range(KW)
    ]
    return jnp.stack(pieces, axis=1)


def square_shards(dna_bases, w_stem, w_enc, w_dec, targets):
    rows = dna_bases.shape[0]
    n = lax.axis_size("seq")
    length = rows * n
    s = lax.axis_index("seq")
    c1, c2 = w_stem.shape[0], w_dec.shape[2]
    struct = jax.ShapeDtypeStruct
    bases = call(
        functools.partial(bases_kernel, n), 0, struct((n, rows // 128, 128), jnp.int32),
        [pltpu.SemaphoreType.DMA, dma(n - 1), dma(n - 1)], dna_bases.reshape(rows // 128, 128),
    ).reshape(length)
    bases_pad = jnp.pad(bases, (2, 2), constant_values=-1)
    shifts = jnp.stack([bases_pad[k : k + length] for k in range(KW)])
    onehot = (shifts[:, None, :] == jnp.arange(4, dtype=jnp.int32)[None, :, None]).astype(BF16)
    stem_pre = lax.dot_general(
        onehot.reshape(KW * 4, length), w_stem.reshape(c1, KW * 4), (((0,), (1,)), ((), ())),
        preferred_element_type=jnp.float32,
    )
    stem_all = jnp.pad(gelu_value(stem_pre).astype(BF16), ((2, 2), (0, 0)))
    stem_pad = lax.dynamic_slice_in_dim(stem_all, s * rows, rows + 4, 0)
    part = conv_stack(stem_pad, w_enc).astype(BF16)
    half = rows // 2
    enc_pre, up_own, pool = call(
        functools.partial(encoder_kernel, n), 1,
        (
            struct((rows, c2), jnp.float32),
            struct((rows + 2 * EDGE, c2), BF16),
            struct((half, c2), BF16),
        ),
        [
            pltpu.VMEM((n - 1, rows, c2), BF16),
            pltpu.VMEM((rows, c2), BF16),
            pltpu.VMEM((c2 // 128, rows, 128), jnp.float32),
            dma(3 * CHUNKS), dma(3 * CHUNKS), dma(2), dma(2),
        ],
        part,
    )
    up_pad = up_own[EDGE - 2 : EDGE + rows + 2]
    dec_part = jnp.stack(
        [conv_stack(up_pad, w_dec[j * c1 : (j + 1) * c1]).astype(BF16) for j in range(n)]
    )
    pred, slope_chan, pool_all = call(
        functools.partial(slope_kernel, n, 1.0 / math.sqrt(length)), 2,
        (
            struct((rows, c1), BF16),
            struct((n, rows + 2 * EDGE, c1), BF16),
            struct((n, half, c2), BF16),
        ),
        [
            pltpu.VMEM((n - 1, rows, c1), BF16),
            pltpu.VMEM((rows, c1), BF16),
            dma(3 * CHUNKS), dma(3 * CHUNKS), dma(3 * CHUNKS), dma(3 * CHUNKS),
            dma(n), dma(n), dma(n), dma(n), dma(n), dma(n), dma(n),
            pltpu.SemaphoreType.DMA,
        ],
        dec_part, stem_pad[2 : 2 + rows], targets, pool,
    )
    pre_seq, slope_seq, up_all = call(
        functools.partial(turn_kernel, n), 3,
        (
            struct((n, rows, c2), BF16),
            struct((n, rows, c1), BF16),
            struct((n, rows, c2), BF16),
        ),
        [
            pltpu.VMEM((rows, c2), BF16),
            pltpu.VMEM((c2 // 128, rows, 128), jnp.float32),
            pltpu.VMEM((rows // n, c2), jnp.float32),
            *turn_scratch(n), *turn_scratch(n),
        ],
        w_dec.transpose(1, 0, 2), enc_pre, slope_chan, pool_all,
    )
    up_all = jnp.pad(up_all.reshape(length, c2), ((2, 2), (0, 0)))
    g_dec = all_rows_grad(slope_seq.reshape(length, c1), up_all)
    g_enc = all_rows_grad(pre_seq.reshape(length, c2), stem_all)
    return (pred, g_enc, g_dec)


def shards(dna_bases, w_stem, w_enc, w_dec, targets):
    args = (dna_bases, w_stem, w_enc, w_dec, targets)
    rows, c1, c2 = dna_bases.shape[0], w_stem.shape[0], w_dec.shape[2]
    n = lax.axis_size("seq")
    square = n == 4 and lax.axis_size("chan") == 4
    if square and rows % (CHUNKS * STEP) == 0 and c2 % 128 == 0 and c1 % 64 == 0:
        return square_shards(*args)
    return general_shards(*args)


def solution(mesh):
    return jax.shard_map(
        shards,
        mesh=mesh,
        in_specs=(
            P(("groups", "seq")),
            P("chan", None, None),
            P(None, None, "chan"),
            P(None, None, "chan"),
            P(("groups", "seq"), "chan"),
        ),
        out_specs=(
            P(("groups", "seq"), "chan"),
            P(("groups", "seq"), None, "chan"),
            P(("groups", "seq"), None, "chan"),
        ),
        check_vma=False,
    )
```

```python
import functools
import math

import jax
import jax.numpy as jnp
from jax import lax
from jax.experimental import pallas as pl
from jax.experimental.pallas import tpu as pltpu
from jax.sharding import PartitionSpec as P

KW = 5


SQRT_TWO_PI = 0.7978845608028654
CUBIC = 0.044715


def extended(block, sides, width):
    for axis, dim in sides:
        count = lax.axis_size(axis)
        forward = [(i, i + 1) for i in range(count - 1)]
        backward = [(target, source) for source, target in forward]
        low = lax.ppermute(
            lax.slice_in_dim(block, block.shape[dim] - width, None, axis=dim), axis, forward
        )
        high = lax.ppermute(lax.slice_in_dim(block, 0, width, axis=dim), axis, backward)
        block = jnp.concatenate([low, block, high], axis=dim)
    return block


def gelu_value(value):
    inner = jnp.tanh(SQRT_TWO_PI * (value + CUBIC * value * value * value))
    return 0.5 * value * (1.0 + inner)


def gelu_slope(value):
    inner = jnp.tanh(SQRT_TWO_PI * (value + CUBIC * value * value * value))
    return 0.5 * (1.0 + inner) + 0.5 * value * (1.0 - inner * inner) * SQRT_TWO_PI * (
        1.0 + 3.0 * CUBIC * value * value
    )


def rim_cells(block, margin):
    return extended(block, (("seq", 0),), margin)


def channel_sum(partial_value):
    return lax.psum_scatter(partial_value, "chan", scatter_dimension=1, tiled=True)


def channel_gather(block):
    return lax.all_gather(block, "chan", axis=1, tiled=True)


def conv_rows(padded, weight):
    row_count = padded.shape[0] - 4
    total = jnp.zeros((row_count, weight.shape[0]), jnp.float32)
    for k in range(KW):
        total = total + lax.dot_general(
            padded[k : k + row_count],
            weight[:, k, :],
            (((1,), (1,)), ((), ())),
            preferred_element_type=jnp.float32,
        )
    return total


def grad_taps(picked, padded):
    row_count = picked.shape[0]
    pieces = [
        lax.dot_general(
            picked,
            padded[k : k + row_count],
            (((0,), (0,)), ((), ())),
            preferred_element_type=jnp.float32,
        )
        for k in range(KW)
    ]
    return jnp.stack(pieces, axis=1)


def weight_grad(cotangent, padded):
    rounded = grad_taps(cotangent, padded).astype(jnp.bfloat16)
    return lax.psum_scatter(
        lax.optimization_barrier(rounded).astype(jnp.float32),
        "seq",
        scatter_dimension=0,
        tiled=True,
    )


def general_shards(dna_bases, w_stem, w_enc, w_dec, targets):
    row_count = dna_bases.shape[0]
    devices = lax.axis_size("seq")
    length = row_count * devices
    onehot = (dna_bases[:, None] == jnp.arange(4, dtype=jnp.int32)[None, :]).astype(jnp.bfloat16)
    onehot_pad = rim_cells(onehot, 2)
    stem_out = gelu_value(conv_rows(onehot_pad, w_stem)).astype(jnp.bfloat16)
    stem_pad = rim_cells(stem_out, 2)
    enc_pre = channel_sum(conv_rows(stem_pad, w_enc))
    active = gelu_value(enc_pre).astype(jnp.bfloat16).astype(jnp.float32)
    pooled = (0.5 * active.reshape(row_count // 2, 2, -1).sum(axis=1)).astype(jnp.bfloat16)
    pooled_pad = rim_cells(pooled, 1)
    up_pad = jnp.repeat(pooled_pad, 2, axis=0)
    output = channel_sum(conv_rows(up_pad, w_dec)) + stem_out.astype(jnp.float32)
    pred = output.astype(jnp.bfloat16)
    scale = 1.0 / math.sqrt(length)
    slope_out = ((output - targets.astype(jnp.float32)) * scale).astype(jnp.bfloat16)
    slope_all = channel_gather(slope_out)
    g_dec = weight_grad(slope_all, up_pad)
    slope_pad = rim_cells(slope_all, 2)
    up_grad = jnp.zeros((row_count, w_dec.shape[2]), jnp.float32)
    for k in range(KW):
        up_grad = up_grad + jnp.dot(
            slope_pad[4 - k : 4 - k + row_count], w_dec[:, k, :], preferred_element_type=jnp.float32
        )
    pool_grad = up_grad.reshape(row_count // 2, 2, -1).sum(axis=1)
    act_grad = 0.5 * jnp.repeat(pool_grad, 2, axis=0)
    pre_grad = (act_grad * gelu_slope(enc_pre)).astype(jnp.bfloat16)
    pre_all = channel_gather(pre_grad)
    g_enc = weight_grad(pre_all, stem_pad)
    return (pred, g_enc, g_dec)


MESH_ID = pl.DeviceIdType.MESH
BF16 = jnp.bfloat16
EDGE = 16
CHUNKS = 4
STEP = 64
VMEM_BYTES = 8 * 1024 * 1024


def send(src, dst, send_sem, recv_sem, seq, chan):
    return pltpu.make_async_remote_copy(
        src_ref=src,
        dst_ref=dst,
        send_sem=send_sem,
        recv_sem=recv_sem,
        device_id={"seq": seq, "chan": chan},
        device_id_type=MESH_ID,
    )


def greet(targets):
    barrier = pltpu.get_barrier_semaphore()
    for seq, chan in targets:
        pl.semaphore_signal(
            barrier, inc=1, device_id={"seq": seq, "chan": chan}, device_id_type=MESH_ID
        )
    pl.semaphore_wait(barrier, len(targets))


def whole_group(n, s, c):
    others = []
    for ds in range(n):
        for dc in range(n):
            if ds or dc:
                others.append((lax.rem(s + ds, n), lax.rem(c + dc, n)))
    return others


def bases_kernel(n, own_ref, all_ref, local_sem, send_sem, recv_sem):
    s, c = lax.axis_index("seq"), lax.axis_index("chan")
    peers = [lax.rem(s + d, n) for d in range(1, n)]
    greet([(p, c) for p in peers])
    copies = [
        send(own_ref, all_ref.at[s], send_sem.at[d], recv_sem.at[d], p, c)
        for d, p in enumerate(peers)
    ]
    for copy in copies:
        copy.start()
    mine = pltpu.make_async_copy(own_ref, all_ref.at[s], local_sem)
    mine.start()
    mine.wait()
    for copy in copies:
        copy.wait()


def partners(c):
    mate = c + 1 - 2 * lax.rem(c, 2)
    across = lax.rem(c + 2, 4)
    return mate, across, lax.rem(mate + 2, 4)


class Turn:
    def __init__(self, n, s, c, own, out, sems):
        self.n, self.s, self.c, self.own, self.out = n, s, c, own, out
        self.quarter_send, self.quarter_recv, self.share_send, self.share_recv, self.local = sems
        self.piece = own.shape[0] // n

    def rows(self, index):
        return pl.ds(pl.multiple_of(index * self.piece, self.piece), self.piece)

    def keep(self):
        at = self.rows(self.c)
        return pltpu.make_async_copy(self.own.at[at], self.out.at[self.s, at], self.local)

    def quarter(self, q, slot):
        at = self.rows(q)
        return send(self.own.at[at], self.out.at[self.s, at], self.quarter_send.at[q],
                    self.quarter_recv.at[slot], self.c, q)

    def each(self, action, mine, before=None):
        for q in range(self.n):
            if before is not None:
                before(q * self.piece)
            itself = jnp.logical_and(self.s == self.c, self.c == q)
            pl.when(jnp.logical_not(itself))(functools.partial(action, q))
        if mine is not None:
            pl.when(self.s == self.c)(mine)

    def start(self, before=None):
        self.each(
            lambda q: self.quarter(q, self.s).start(), lambda: self.keep().start(), before
        )

    def share(self, slot, kind, part, to):
        at = self.rows(part)
        index = slot * 3 + kind
        return send(self.out.at[slot, at], self.out.at[slot, at], self.share_send.at[index],
                    self.share_recv.at[index], self.s, to)

    def slots(self):
        return [lax.rem(self.s + d, self.n) for d in range(self.n)]

    def forward(self):
        mate, across, _ = partners(self.c)
        for d, slot in enumerate(self.slots()):
            if d == 0:
                pl.when(self.s == self.c)(lambda: self.keep().wait())
                pl.when(self.s != self.c)(lambda: self.quarter(self.c, slot).wait_recv())
            else:
                self.quarter(self.c, slot).wait_recv()
            self.share(slot, 1, self.c, across).start()
            self.share(slot, 0, self.c, mate).start()

    def relay(self):
        mate, across, _ = partners(self.c)
        for slot in self.slots():
            self.share(slot, 1, across, across).wait_recv()
            self.share(slot, 2, across, mate).start()

    def finish(self):
        mate, across, far = partners(self.c)
        for slot in self.slots():
            self.share(slot, 0, mate, mate).wait_recv()
            self.share(slot, 2, far, mate).wait_recv()
            self.share(slot, 0, self.c, mate).wait_send()
            self.share(slot, 1, self.c, across).wait_send()
            self.share(slot, 2, across, mate).wait_send()
        self.each(lambda q: self.quarter(q, self.s).wait_send(), None)


def pair_sum(block, held, pair, s, c, rows, send_sem, recv_sem, finish, done):
    mate, across, far = partners(c)
    piece = rows // CHUNKS
    sources = (block(mate), block(far), pair)
    targets = (mate, mate, across)

    def hop(kind, q):
        at = pl.ds(q * piece, piece)
        index = kind * CHUNKS + q
        return send(sources[kind].at[at], held.at[kind, at], send_sem.at[index],
                    recv_sem.at[index], s, targets[kind])

    def steps(q, body):
        @pl.loop(0, piece // STEP)
        def _(i):
            body(pl.ds(pl.multiple_of(q * piece + i * STEP, STEP), STEP))

    def pair_rows(at):
        pair[at, :] = (
            block(across)[at, :].astype(jnp.float32) + held[1, at, :].astype(jnp.float32)
        ).astype(BF16)

    def total_rows(at):
        total = block(c)[at, :].astype(jnp.float32) + held[0, at, :].astype(jnp.float32)
        finish(at, total + held[2, at, :].astype(jnp.float32))

    for q in range(CHUNKS):
        hop(1, q).start()
    for q in range(CHUNKS):
        hop(0, q).start()
    for q in range(CHUNKS):
        hop(1, q).wait_recv()
        steps(q, pair_rows)
        hop(2, q).start()
    for q in range(CHUNKS):
        hop(0, q).wait_recv()
        hop(2, q).wait_recv()
        steps(q, total_rows)
        done(q)
    return [hop(kind, q) for kind in range(3) for q in range(CHUNKS)]


def pair_add(value):
    count = value.shape[0]
    row = lax.broadcasted_iota(jnp.int32, value.shape, 0)
    other = jnp.where(
        lax.rem(row, 2) == 0, pltpu.roll(value, count - 1, 0), pltpu.roll(value, 1, 0)
    )
    return value + other


def encoder_kernel(
    n, part_ref, pre_ref, up_ref, pool_ref, held, pair, wide,
    send_sem, recv_sem, edge_send, edge_recv,
):
    s, c = lax.axis_index("seq"), lax.axis_index("chan")
    rows, width = pre_ref.shape
    half = rows // 2
    greet(
        [(s, lax.rem(c + d, n)) for d in range(1, n)]
        + [(lax.rem(s + d, n), c) for d in range(1, n)]
    )

    def block(j):
        return part_ref.at[:, pl.ds(pl.multiple_of(j * width, 128), width)]

    def finish(at, total):
        pre_ref[at, :] = total
        active = gelu_value(total).astype(BF16).astype(jnp.float32)
        pooled = (0.5 * pair_add(active)).astype(BF16)
        up_ref[pl.ds(pl.multiple_of(at.start + EDGE, EDGE), at.size), :] = pooled
        for j in range(width // 128):
            wide[j, at, :] = pooled[:, j * 128 : (j + 1) * 128].astype(jnp.float32)

    copies = pair_sum(
        block, held, pair, s, c, rows, send_sem, recv_sem, finish, lambda q: None
    )
    up = send(up_ref.at[pl.ds(rows, EDGE)], up_ref.at[pl.ds(0, EDGE)], edge_send.at[0],
              edge_recv.at[0], lax.rem(s + 1, n), c)
    down = send(up_ref.at[pl.ds(EDGE, EDGE)], up_ref.at[pl.ds(rows + EDGE, EDGE)],
                edge_send.at[1], edge_recv.at[1], lax.rem(s + n - 1, n), c)
    up.start()
    down.start()
    for j in range(width // 128):
        pool_ref[:, j * 128 : (j + 1) * 128] = wide[j, pl.ds(0, half, stride=2), :].astype(BF16)
    up.wait()
    down.wait()
    blank = jnp.zeros((EDGE, width), BF16)

    @pl.when(s == 0)
    def _():
        up_ref[0:EDGE, :] = blank

    @pl.when(s == n - 1)
    def _():
        up_ref[rows + EDGE :, :] = blank

    for copy in copies:
        copy.wait_send()


class PoolRelay:
    def __init__(self, n, s, c, own, out, right_send, left_send, recv, local):
        self.n, self.s, self.c, self.own, self.out = n, s, c, own, out
        self.right_send, self.left_send, self.recv = right_send, left_send, recv
        self.mine = pltpu.make_async_copy(own, out.at[s], local)

    def hop(self, src, slot, step):
        sems = self.right_send if step > 0 else self.left_send
        return send(src, self.out.at[slot], sems.at[slot], self.recv.at[slot], self.s + step, self.c)

    def start(self):
        pl.when(self.s < self.n - 1)(lambda: self.hop(self.own, self.s, 1).start())
        pl.when(self.s > 0)(lambda: self.hop(self.own, self.s, -1).start())
        self.mine.start()

    def arrive(self, d):
        low, high = self.s - d, self.s + d

        @pl.when(low >= 0)
        def _():
            self.hop(self.out.at[low], low, 1).wait_recv()
            pl.when(self.s < self.n - 1)(lambda: self.hop(self.out.at[low], low, 1).start())

        @pl.when(high < self.n)
        def _():
            self.hop(self.out.at[high], high, -1).wait_recv()
            pl.when(self.s > 0)(lambda: self.hop(self.out.at[high], high, -1).start())

    def end(self):
        self.mine.wait()
        for slot in range(self.n):
            pl.when(jnp.logical_and(slot <= self.s, self.s < self.n - 1))(
                lambda: self.hop(self.own, slot, 1).wait_send()
            )
            pl.when(jnp.logical_and(slot >= self.s, self.s > 0))(
                lambda: self.hop(self.own, slot, -1).wait_send()
            )


def slope_kernel(
    n, scale, part_ref, stem_ref, target_ref, pool_ref, pred_ref, chan_ref, all_ref,
    held, pair, send_sem, recv_sem, row_send, row_recv, lo_send, lo_recv, hi_send, hi_recv,
    right_send, left_send, pool_recv, local_sem,
):
    s, c = lax.axis_index("seq"), lax.axis_index("chan")
    rows, width = pred_ref.shape
    piece = rows // CHUNKS
    mate, across, far = partners(c)
    greet(whole_group(n, s, c))
    pools = PoolRelay(n, s, c, pool_ref, all_ref, right_send, left_send, pool_recv, local_sem)
    up, down = lax.rem(s + 1, n), lax.rem(s + n - 1, n)

    def finish(at, total):
        output = total + stem_ref[at, :].astype(jnp.float32)
        pred_ref[at, :] = output.astype(BF16)
        spot = pl.ds(pl.multiple_of(at.start + EDGE, EDGE), at.size)
        chan_ref[c, spot, :] = ((output - target_ref[at, :].astype(jnp.float32)) * scale).astype(BF16)

    def row_copy(kind, q, owner, to):
        spot = chan_ref.at[owner, pl.ds(EDGE + q * piece, piece)]
        index = kind * CHUNKS + q
        return send(spot, spot, row_send.at[index], row_recv.at[index], s, to)

    lo_copies, hi_copies = [], []
    for d in range(n):
        p = lax.rem(c + d, n)
        lo_copies.append(
            send(chan_ref.at[c, pl.ds(rows, EDGE)], chan_ref.at[c, pl.ds(0, EDGE)],
                 lo_send.at[d], lo_recv.at[d], up, p)
        )
        hi_copies.append(
            send(chan_ref.at[c, pl.ds(EDGE, EDGE)], chan_ref.at[c, pl.ds(EDGE + rows, EDGE)],
                 hi_send.at[d], hi_recv.at[d], down, p)
        )

    def done(q):
        row_copy(1, q, c, across).start()
        row_copy(0, q, c, mate).start()
        if q == 0:
            for copy in hi_copies:
                copy.start()
        if q == CHUNKS - 1:
            for copy in lo_copies:
                copy.start()

    pools.start()
    copies = pair_sum(
        lambda j: part_ref.at[j], held, pair, s, c, rows, send_sem, recv_sem, finish, done
    )
    pools.arrive(1)
    for q in range(CHUNKS):
        row_copy(1, q, across, across).wait_recv()
        row_copy(2, q, across, mate).start()
    pools.arrive(2)
    for q in range(CHUNKS):
        row_copy(0, q, mate, mate).wait_recv()
        row_copy(2, q, far, mate).wait_recv()
    for copy in lo_copies + hi_copies:
        copy.wait()
    blank = jnp.zeros((EDGE, width), BF16)

    @pl.when(s == 0)
    def _():
        for j in range(n):
            chan_ref[j, 0:EDGE, :] = blank

    @pl.when(s == n - 1)
    def _():
        for j in range(n):
            chan_ref[j, EDGE + rows :, :] = blank

    pools.arrive(3)
    pools.end()
    for q in range(CHUNKS):
        row_copy(0, q, c, mate).wait_send()
        row_copy(1, q, c, across).wait_send()
        row_copy(2, q, across, mate).wait_send()
    for copy in copies:
        copy.wait_send()


def turn_kernel(
    n, w_ref, pre_ref, chan_ref, all_ref, pre_seq_ref, slope_seq_ref, up_ref, own, wide, total,
    *sems,
):
    s, c = lax.axis_index("seq"), lax.axis_index("chan")
    rows = own.shape[0]
    half, up_width = all_ref.shape[1:]
    slope_own = chan_ref.at[c, pl.ds(EDGE, rows)]
    slope_turn = Turn(n, s, c, slope_own, slope_seq_ref, sems[: len(sems) // 2])
    turn = Turn(n, s, c, own, pre_seq_ref, sems[len(sems) // 2 :])

    width = chan_ref.shape[2]
    piece = turn.piece

    def pre_rows(first):
        if first == 2 * piece:
            slope_turn.forward()
        if first == 3 * piece:
            slope_turn.relay()
        total[...] = jnp.zeros_like(total)

        @pl.loop(0, n)
        def _(j):
            window = chan_ref[j, first : first + piece + 2 * EDGE, :].astype(jnp.float32)
            inputs = pl.ds(pl.multiple_of(j * width, EDGE), width)
            part = total[...]
            for k in range(KW):
                start = EDGE + 2 - k
                part = part + jnp.dot(
                    window[start : start + piece].astype(BF16), w_ref[k, inputs, :],
                    preferred_element_type=jnp.float32,
                )
            total[...] = part

        @pl.loop(0, piece // STEP)
        def _(i):
            local = pl.ds(pl.multiple_of(i * STEP, STEP), STEP)
            at = pl.ds(pl.multiple_of(first + i * STEP, STEP), STEP)
            grad = 0.5 * pair_add(total[local, :])
            own[at, :] = (grad * gelu_slope(pre_ref[at, :])).astype(BF16)

    slope_turn.start()
    turn.start(pre_rows)
    turn.forward()

    @pl.loop(0, n)
    def _(slot):
        for j in range(up_width // 128):
            lanes = slice(j * 128, (j + 1) * 128)
            value = all_ref[slot, :, lanes].astype(jnp.float32)
            wide[j, pl.ds(0, half, stride=2), :] = value
            wide[j, pl.ds(1, half, stride=2), :] = value
            up_ref[slot, :, lanes] = wide[j].astype(BF16)

    turn.relay()
    slope_turn.finish()
    turn.finish()


def decoder_kernel(
    n, scale, part_ref, stem_ref, target_ref, pool_ref, w_ref, pre_ref,
    pred_ref, pre_seq_ref, slope_seq_ref, up_ref, chan, pools, held, pair, own, wide, total, *sems
):
    slope_kernel(
        n, scale, part_ref, stem_ref, target_ref, pool_ref, pred_ref, chan, pools, held, pair,
        *sems[:12],
    )
    turn_kernel(
        n, w_ref, pre_ref, chan, pools, pre_seq_ref, slope_seq_ref, up_ref, own, wide, total,
        *sems[12:],
    )


def turn_scratch(n):
    return [dma(n), dma(n), dma(3 * n), dma(3 * n), pltpu.SemaphoreType.DMA]


def call(kernel, ident, outs, scratch, *operands):
    vmem = pl.BlockSpec(memory_space=pltpu.VMEM)
    return pl.pallas_call(
        kernel,
        out_shape=outs,
        in_specs=[vmem] * len(operands),
        out_specs=jax.tree.map(lambda _: vmem, outs),
        scratch_shapes=scratch,
        compiler_params=pltpu.CompilerParams(
            collective_id=ident, has_side_effects=True, vmem_limit_bytes=VMEM_BYTES
        ),
    )(*operands)


def dma(count):
    return pltpu.SemaphoreType.DMA((count,))


def windows(padded):
    count = padded.shape[0] - 4
    return jnp.stack([padded[k : k + count] for k in range(KW)], axis=0)


def conv_stack(padded, weight):
    return lax.dot_general(
        windows(padded), weight, (((0, 2), (1, 2)), ((), ())), preferred_element_type=jnp.float32
    )


def all_rows_grad(cotangent, padded):
    count = cotangent.shape[0]
    pieces = [
        lax.dot_general(
            cotangent, padded[k : k + count], (((0,), (0,)), ((), ())),
            preferred_element_type=jnp.float32,
        )
        for k in range(KW)
    ]
    return jnp.stack(pieces, axis=1)


def square_shards(dna_bases, w_stem, w_enc, w_dec, targets):
    rows = dna_bases.shape[0]
    n = lax.axis_size("seq")
    length = rows * n
    s = lax.axis_index("seq")
    c1, c2 = w_stem.shape[0], w_dec.shape[2]
    struct = jax.ShapeDtypeStruct
    bases = call(
        functools.partial(bases_kernel, n), 0, struct((n, rows // 128, 128), jnp.int32),
        [pltpu.SemaphoreType.DMA, dma(n - 1), dma(n - 1)], dna_bases.reshape(rows // 128, 128),
    ).reshape(length)
    bases_pad = jnp.pad(bases, (2, 2), constant_values=-1)
    shifts = jnp.stack([bases_pad[k : k + length] for k in range(KW)])
    onehot = (shifts[:, None, :] == jnp.arange(4, dtype=jnp.int32)[None, :, None]).astype(BF16)
    stem_pre = lax.dot_general(
        onehot.reshape(KW * 4, length), w_stem.reshape(c1, KW * 4), (((0,), (1,)), ((), ())),
        preferred_element_type=jnp.float32,
    )
    stem_all = jnp.pad(gelu_value(stem_pre).astype(BF16), ((2, 2), (0, 0)))
    stem_pad = lax.dynamic_slice_in_dim(stem_all, s * rows, rows + 4, 0)
    part = conv_stack(stem_pad, w_enc).astype(BF16)
    half = rows // 2
    enc_pre, up_own, pool = call(
        functools.partial(encoder_kernel, n), 1,
        (
            struct((rows, c2), jnp.float32),
            struct((rows + 2 * EDGE, c2), BF16),
            struct((half, c2), BF16),
        ),
        [
            pltpu.VMEM((n - 1, rows, c2), BF16),
            pltpu.VMEM((rows, c2), BF16),
            pltpu.VMEM((c2 // 128, rows, 128), jnp.float32),
            dma(3 * CHUNKS), dma(3 * CHUNKS), dma(2), dma(2),
        ],
        part,
    )
    up_pad = up_own[EDGE - 2 : EDGE + rows + 2]
    dec_part = jnp.stack(
        [conv_stack(up_pad, w_dec[j * c1 : (j + 1) * c1]).astype(BF16) for j in range(n)]
    )
    pred, pre_seq, slope_seq, up_all = call(
        functools.partial(decoder_kernel, n, 1.0 / math.sqrt(length)), 2,
        (
            struct((rows, c1), BF16),
            struct((n, rows, c2), BF16),
            struct((n, rows, c1), BF16),
            struct((n, rows, c2), BF16),
        ),
        [
            pltpu.VMEM((n, rows + 2 * EDGE, c1), BF16),
            pltpu.VMEM((n, half, c2), BF16),
            pltpu.VMEM((n - 1, rows, c1), BF16),
            pltpu.VMEM((rows, c1), BF16),
            pltpu.VMEM((rows, c2), BF16),
            pltpu.VMEM((c2 // 128, rows, 128), jnp.float32),
            pltpu.VMEM((rows // n, c2), jnp.float32),
            dma(3 * CHUNKS), dma(3 * CHUNKS), dma(3 * CHUNKS), dma(3 * CHUNKS),
            dma(n), dma(n), dma(n), dma(n), dma(n), dma(n), dma(n),
            pltpu.SemaphoreType.DMA,
            *turn_scratch(n), *turn_scratch(n),
        ],
        dec_part, stem_pad[2 : 2 + rows], targets, pool, w_dec.transpose(1, 0, 2), enc_pre,
    )
    up_all = jnp.pad(up_all.reshape(length, c2), ((2, 2), (0, 0)))
    g_dec = all_rows_grad(slope_seq.reshape(length, c1), up_all)
    g_enc = all_rows_grad(pre_seq.reshape(length, c2), stem_all)
    return (pred, g_enc, g_dec)


def shards(dna_bases, w_stem, w_enc, w_dec, targets):
    args = (dna_bases, w_stem, w_enc, w_dec, targets)
    rows, c1, c2 = dna_bases.shape[0], w_stem.shape[0], w_dec.shape[2]
    n = lax.axis_size("seq")
    square = n == 4 and lax.axis_size("chan") == 4
    if square and rows % (CHUNKS * STEP) == 0 and c2 % 128 == 0 and c1 % 64 == 0:
        return square_shards(*args)
    return general_shards(*args)


def solution(mesh):
    return jax.shard_map(
        shards,
        mesh=mesh,
        in_specs=(
            P(("groups", "seq")),
            P("chan", None, None),
            P(None, None, "chan"),
            P(None, None, "chan"),
            P(("groups", "seq"), "chan"),
        ),
        out_specs=(
            P(("groups", "seq"), "chan"),
            P(("groups", "seq"), None, "chan"),
            P(("groups", "seq"), None, "chan"),
        ),
        check_vma=False,
    )
```
